32 devices in a mesh: win: 2 (over x), gx: 8 (over z, y), gy: 2 (over core).
Axes of the slice: x: 2, y: 2, z: 4, core: 2. Of those that a mesh axis runs over, the one named last changes fastest.
Arguments:
- mask_init: float32 [2048, 256], P(('win', 'gx'), 'gy'), parts along dimension 0, may hold values from 0 to 1
- target_map: int32 [2048, 256], P(('win', 'gx'), 'gy'), parts along dimension 0, may hold values 0 or 1
- kernels: float32 [6, 129, 129], replicated, may hold values from -0.07 to 0.07, as said below
Outputs:
- mask_out: float32 [2048, 256], P(('win', 'gx'), 'gy'), parts along dimension 0
- resist_out: float32 [2048, 256], P(('win', 'gx'), 'gy'), parts along dimension 0
The draws below stay inside these ranges and needn't reach their ends.
There are 2 independent parts, one for each index of `win`. The reference program is written for one: setup_inputs(seed, part) draws one part's arguments, and reference() takes and returns one part's arrays. A program takes and returns all parts, laid end to end along the dimension named above; an argument that names none is the same for every part. Nothing has to cross between parts.
Inputs may be any that keep to these rules, and one draw needn't show every extreme that they name: Each kernel is even: kernels[k, a, b] = kernels[k, 128 - a, 128 - b].
All inputs are finite; a program needn't handle non-finite values. No bound on the sum of `target_map` on one device may be relied on, other than what follows from the above.
Results may differ from the reference program's by a relative error of at most 0.0001.
Values sent between devices are 32-bit elements; how exact they have to be, the bound alone decides.
No kernel may reach another device: no remote copies, remote signals or barrier semaphores. Data moves between devices by JAX's collectives and lax.ppermute only.
A program may use at most 64 MiB of HBM per device.

```python
import jax
import jax.numpy as jnp

KS = 129
NK = 6
ITERS = 2
HX = 1024
HY = 256


def draw_kernels(key, part):
    raw_draw = jnp.clip(jax.random.normal(key, (NK, KS, KS), jnp.float32), -6.0, 6.0)
    mirrored = raw_draw[:, ::-1, ::-1]
    scaled = (raw_draw + mirrored) * (0.70710678 / KS)
    return jnp.clip(scaled, -0.07, 0.07)


def place_ends(values, rng, smallest, largest):
    dims = values.shape
    index_at = [jax.random.randint(jax.random.fold_in(rng, axis), (), 0, dims[axis]) for axis in range(len(dims))]
    values = values.at[tuple(index_at)].set(smallest)
    longest = dims.index(max(dims))
    index_at[longest] = (index_at[longest] + 1) % dims[longest]
    return values.at[tuple(index_at)].set(largest)


def steps_of(stream_key, shape, split, smallest, largest):
    level = 1.0
    for position, blocks in split:
        steps = jax.random.uniform(jax.random.fold_in(jax.random.fold_in(stream_key, 6), position), (blocks,), jnp.float32, smallest / len(split), largest / len(split))
        level = level * jnp.repeat(jnp.exp(steps), shape[position] // blocks).reshape((-1,) + (1,) * (len(shape) - 1 - position))
    return level


def setup_inputs(seed: int = 0, part: int = 0) -> dict:
    key_list = jax.random.split(jax.random.key(seed), 4)
    part_keys = jax.random.split(jax.random.fold_in(key_list[3], part), 4)
    mask_init = jnp.clip(1.0 * jax.random.uniform(part_keys[0], (HX, HY), jnp.float32) ** steps_of(part_keys[0], (HX, HY), ((0, 8), (1, 2)), -0.2, 0.2), 0.0, 1.0)
    target_map = place_ends((jax.random.randint(part_keys[1], (HX, HY), 0, 2) < 1).astype(jnp.int32), jax.random.fold_in(part_keys[1], 1), 0, 1)
    kernels = draw_kernels(jax.random.fold_in(key_list[3], 71), part)
    return dict(mask_init=mask_init, target_map=target_map, kernels=kernels)


step_rate = 0.1
steepness = 4.0
threshold = 1.5


def reference(mask_init, target_map, kernels):
    rim_size = (KS - 1) // 2
    full_x = HX + KS - 1
    full_y = HY + KS - 1
    kernel_spec = jnp.fft.rfft2(kernels, s=(full_x, full_y))
    target_real = target_map.astype(jnp.float32)
    field_now = mask_init
    resist = jnp.zeros_like(mask_init)
    for iteration in range(ITERS):
        padded = jnp.pad(field_now, rim_size)
        field_spec = jnp.fft.rfft2(padded)
        field_magnitude = jnp.fft.irfft2(jnp.conj(kernel_spec) * field_spec[None], s=(full_x, full_y))[:, :HX, :HY]
        intensity = jnp.sum(field_magnitude * field_magnitude, axis=0)
        resist = 1.0 / (1.0 + jnp.exp(-steepness * (intensity - threshold)))
        slope_map = 2.0 * (resist - target_real) * steepness * resist * (1.0 - resist)
        weighted = 2.0 * field_magnitude * slope_map[None]
        weight_spec = jnp.fft.rfft2(weighted, s=(full_x, full_y))
        spread = jnp.fft.irfft2(jnp.sum(kernel_spec * weight_spec, axis=0), s=(full_x, full_y))
        gradient = spread[rim_size:rim_size + HX, rim_size:rim_size + HY]
        field_now = field_now - step_rate * gradient
    return field_now, resist
```

```python
import functools

import jax
import jax.numpy as jnp
import ml_dtypes
import numpy as np
from jax import lax
from jax.experimental import pallas as pl
from jax.experimental.pallas import tpu as pltpu
from jax.sharding import PartitionSpec as P

STEP = 0.1
STEEP = 4.0
THRESHOLD = 1.5
N = 256
H = 128
R = 64
VMEM = pl.BlockSpec(memory_space=pltpu.VMEM)
SMEM = pl.BlockSpec(memory_space=pltpu.SMEM)


def pair(table):
    high = table.astype(np.float32).astype(ml_dtypes.bfloat16)
    low = (table - high.astype(np.float64)).astype(np.float32).astype(ml_dtypes.bfloat16)
    return high, low


def wave_tables():
    place = np.arange(N)
    freq = np.arange(H)
    angle = 2.0 * np.pi * ((freq[:, None] * place[None, :]) % N) / N
    forward = np.concatenate([np.cos(angle), np.sin(angle)], 0)
    forward[H] = np.where(place % 2 == 0, 1.0, -1.0)
    weight = np.full((N,), 2.0)
    weight[0] = weight[H] = 1.0
    inverse = (forward * weight[:, None] / N).T
    return forward, inverse


def spectrum_tables(size, rows):
    slot = np.arange(N)
    freq = np.where(slot < H, slot, np.where(slot == H, H, slot - H))
    b = np.arange(size) - (size - 1) // 2
    right = np.zeros((N, N + H))
    right[:size, :N] = np.cos(2.0 * np.pi * ((b[:, None] * freq[None, :]) % N) / N)
    right[:size, N:] = np.sin(2.0 * np.pi * ((b[:, None] * slot[None, :H]) % N) / N)
    a = np.arange((size + 1) // 2)
    fold = np.where(a == 0, 1.0, 2.0)
    left_cos = np.zeros((N, rows))
    left_cos[:, : a.size] = fold * np.cos(2.0 * np.pi * ((freq[:, None] * a[None, :]) % N) / N)
    left_sin = np.zeros((H, rows))
    left_sin[:, : a.size] = fold * np.sin(2.0 * np.pi * ((slot[:H, None] * a[None, :]) % N) / N)
    return right, left_cos, left_sin


def split(value):
    high = value.astype(jnp.bfloat16)
    low = (value - high.astype(jnp.float32)).astype(jnp.bfloat16)
    return high, low


def dot(left, right):
    return jnp.dot(left, right, preferred_element_type=jnp.float32)


def dot3(left, right):
    return dot(left[0], right[0]) + dot(left[0], right[1]) + dot(left[1], right[0])


def mix(f, p_ref, q_ref, k):
    q = q_ref[k]
    cc, cs, sc, ss = f[:H, :H], f[:H, H:], f[H:, :H], f[H:, H:]
    return (
        p_ref[k, :H, :H] * cc + q * ss,
        p_ref[k, :H, H:] * cs - q * sc,
        p_ref[k, H:, :H] * sc - q * cs,
        p_ref[k, H:, H:] * ss + q * cc,
    )


QUADS = ((0, 0), (0, H), (H, 0), (H, H))


def amplitudes(blocks, field, p_ref, q_ref, t, f_sc, g_sc, h_sc, a_sc, core):
    ey = split(dot3(split(field), (t["ft_h"][...], t["ft_l"][...])))
    fwd = (t["f_h"][...], t["f_l"][...])
    for b in range(blocks):
        rows = slice(b * H, b * H + N)
        f_sc[b] = dot3(fwd, (ey[0][rows], ey[1][rows]))

    def body(k, carry):
        for b in range(blocks):
            parts = mix(f_sc[b], p_ref, q_ref, k)
            for (x, y), part in zip(QUADS, parts):
                high, low = split(part)
                g_sc[x : x + H, y : y + H] = high
                g_sc[N + x : N + x + H, y : y + H] = low
            out = dot(g_sc[...], t["iy"][core])
            h = out[:N, :H] + out[:N, H:] + out[N:, :H]
            high, low = split(h)
            h_sc[0, :, b * H : (b + 1) * H] = high
            h_sc[1, :, b * H : (b + 1) * H] = low
        for c in range(0, blocks, 2):
            cols = slice(c * H, c * H + N)
            both = dot(t["ix"][...], h_sc[0, :, cols])
            out = both[:H] + both[H:] + dot(t["ix"][:H], h_sc[1, :, cols])
            a_sc[k, c * H : (c + 1) * H, :] = out[:, :H]
            a_sc[k, (c + 1) * H : (c + 2) * H, :] = out[:, H:]
        return carry

    lax.fori_loop(0, p_ref.shape[0], body, 0)


def slopes(rows, count, a_sc, target, inside, w_sc):
    total = a_sc[0, :rows, :] * a_sc[0, :rows, :]
    for k in range(1, count):
        total = total + a_sc[k, :rows, :] * a_sc[k, :rows, :]
    resist = 1.0 / (1.0 + jnp.exp(-STEEP * (total - THRESHOLD)))
    slope = 2.0 * (resist - target) * STEEP * resist * (1.0 - resist)
    slope = jnp.where(inside, 2.0 * slope, 0.0)
    for k in range(count):
        high, low = split(a_sc[k, :rows, :] * slope)
        w_sc[k, :rows, :H] = high
        w_sc[k, :rows, H:] = low
    return resist


def gradients(blocks, p_ref, q_ref, t, w_sc, z_sc, core):
    rows = (blocks + 1) * H
    own = pl.ds(pl.multiple_of(core * H, H), H)
    z_sc[...] = jnp.zeros_like(z_sc)

    def body(k, carry):
        w = w_sc[k, :rows, :]
        wy = dot(w, t["fy_hh"][core]) + dot(w[:, :H], t["ft_l"][own, :])
        high, low = split(wy)
        for b in range(blocks):
            part = slice(b * H, b * H + N)
            f = dot3((t["f_h"][...], t["f_l"][...]), (high[part], low[part]))
            for (x, y), part in zip(QUADS, mix(f, p_ref, q_ref, k)):
                z_sc[b, x : x + H, y : y + H] += part
        return carry

    lax.fori_loop(0, p_ref.shape[0], body, 0)
    out = []
    for b in range(blocks):
        high, low = split(z_sc[b])
        both = dot(t["ix"][...], high)
        zx = both[:H] + both[H:] + dot(t["ix"][:H], low)
        out.append(dot3(split(zx), (t["it_h"][...], t["it_l"][...])))
    return out


def lane_mask(shape, core):
    lane = lax.broadcasted_iota(jnp.int32, shape, 1)
    return (lane >= core * R) & (lane < N - R + core * R)


def row_mask(shape, first, total):
    row = lax.broadcasted_iota(jnp.int32, shape, 0) + first
    return (row >= 0) & (row < total)


def spectrum_kernel(k_ref, rh_ref, rl_ref, ch_ref, cl_ref, sh_ref, sl_ref, p_ref, q_ref):
    count = p_ref.shape[0]
    rows = k_ref.shape[0] // count
    section = dot3(split(k_ref[...]), (rh_ref[...], rl_ref[...]))
    for k in range(count):
        high, low = split(section[k * rows : (k + 1) * rows])
        p_ref[k] = dot3((ch_ref[...], cl_ref[...]), (high[:, :N], low[:, :N]))
        q_ref[k] = dot3((sh_ref[...], sl_ref[...]), (high[:, N:], low[:, N:]))


TABLES = ("f_h", "f_l", "ft_h", "ft_l", "it_h", "it_l", "ix", "iy", "fy_hh")


def first_kernel(where_ref, own_ref, s1_ref, r1_ref, s2_ref, r2_ref, p_ref, q_ref, *refs):
    t = dict(zip(TABLES, refs))
    rest_ref, send_ref, target_ref, f_sc, g_sc, h_sc, a_sc, w_sc, z_sc = refs[len(TABLES) :]
    core, tile, total = where_ref[0], where_ref[1], where_ref[2]
    count = p_ref.shape[0]
    low1 = jnp.where(core == 0, s1_ref[...], r1_ref[...])
    upp1 = jnp.where(core == 0, r1_ref[...], s1_ref[...])
    low2 = jnp.where(core == 0, s2_ref[...], r2_ref[...])
    upp2 = jnp.where(core == 0, r2_ref[...], s2_ref[...])
    field = jnp.concatenate([low2[:H], low1[:H], own_ref[:H], upp1[:H], upp2[:H]], 0)
    inside = row_mask(field.shape, (tile - 2) * H, total) & lane_mask(field.shape, core)
    field = jnp.where(inside, field, 0.0)
    target = jnp.concatenate([low2[H:], low1[H:], own_ref[H:], upp1[H:], upp2[H:]], 0)
    target = jnp.where(core == 0, target[:, :H], target[:, H:])
    amplitudes(4, field, p_ref, q_ref, t, f_sc, g_sc, h_sc, a_sc, core)
    slopes(4 * H, count, a_sc, target, row_mask((4 * H, H), (tile - 1) * H - R, total), w_sc)
    target_ref[...] = target[H : 3 * H]
    for b, part in enumerate(gradients(3, p_ref, q_ref, t, w_sc, z_sc, core)):
        rows = slice(b * H, (b + 1) * H)
        rest_ref[rows, :] = field[(b + 1) * H : (b + 2) * H] - STEP * part
        send_ref[rows, :] = pltpu.roll(part, N - R, 1)[:, :H]


def second_kernel(where_ref, rest_ref, got_ref, target_ref, p_ref, q_ref, *refs):
    t = dict(zip(TABLES, refs))
    mask_ref, send_ref, resist_ref, f_sc, g_sc, h_sc, a_sc, w_sc, z_sc = refs[len(TABLES) :]
    core, tile, total = where_ref[0], where_ref[1], where_ref[2]
    count = p_ref.shape[0]
    got = jnp.concatenate([got_ref[...], jnp.zeros_like(got_ref)], 1)
    field = rest_ref[...] - STEP * pltpu.roll(got, R, 1)
    inside = row_mask(field.shape, (tile - 1) * H, total) & lane_mask(field.shape, core)
    field = jnp.where(inside, field, 0.0)
    amplitudes(2, field, p_ref, q_ref, t, f_sc, g_sc, h_sc, a_sc, core)
    inside = row_mask((2 * H, H), tile * H - R, total)
    resist = slopes(2 * H, count, a_sc, target_ref[...], inside, w_sc)
    resist_ref[...] = resist[R : R + H]
    (part,) = gradients(1, p_ref, q_ref, t, w_sc, z_sc, core)
    part = jnp.where(lane_mask(part.shape, core), STEP * part, 0.0)
    own = field[H : 2 * H] - part
    mask_ref[...] = jnp.where(core == 0, own[:, :H], own[:, H:])
    send_ref[...] = jnp.where(core == 0, part[:, H:], part[:, :H])


def shape(*dims, dtype=jnp.float32):
    return jax.ShapeDtypeStruct(dims, dtype)


def scratch(blocks, adjoint_blocks, count):
    return [
        pltpu.VMEM((blocks, N, N), jnp.float32),
        pltpu.VMEM((2 * N, N), jnp.bfloat16),
        pltpu.VMEM((2, N, blocks * H), jnp.bfloat16),
        pltpu.VMEM((count, blocks * H, H), jnp.float32),
        pltpu.VMEM((count, blocks * H, N), jnp.bfloat16),
        pltpu.VMEM((adjoint_blocks, N, N), jnp.float32),
    ]


def per_device(mask_init, target_map, kernels, tiles):
    count, size, _ = kernels.shape
    core = lax.axis_index("gy")
    tile = lax.axis_index("gx")
    swap = [(0, 1), (1, 0)]

    def place(step):
        step %= 2 * tiles
        return 2 * step if step < tiles else 2 * (2 * tiles - 1 - step) + 1

    def ring(shift):
        return [(place(i), place(i + shift)) for i in range(2 * tiles)]

    rows = 72
    half = jnp.pad(
        kernels[:, (size - 1) // 2 :, :],
        ((0, 0), (0, rows - (size + 1) // 2), (0, N - size)),
    ).reshape(count * rows, N)
    spectral = [jnp.asarray(v) for tab in spectrum_tables(size, rows) for v in pair(tab)]
    p, q = pl.pallas_call(
        spectrum_kernel,
        out_shape=(shape(count, N, N), shape(count, H, H)),
        in_specs=[VMEM] * 7,
        out_specs=(VMEM, VMEM),
        cost_estimate=pl.CostEstimate(
            flops=6 * count * rows * N * N * 4, bytes_accessed=4 * count * N * N, transcendentals=0
        ),
        name="spectra",
    )(half, *spectral)

    forward, inverse = wave_tables()
    f_h, f_l = pair(forward)
    i_h, i_l = pair(inverse)
    middle_h, middle_l = i_h[R : R + H], i_l[R : R + H]
    it_h, it_l = np.ascontiguousarray(i_h.T), np.ascontiguousarray(i_l.T)
    ft_h, ft_l = np.ascontiguousarray(f_h.T), np.ascontiguousarray(f_l.T)
    iy = np.stack([np.concatenate([it_h[:, c : c + H], it_l[:, c : c + H]], 1) for c in (0, H)])
    fy_hh = np.stack([np.concatenate([ft_h[c : c + H], ft_h[c : c + H]], 0) for c in (0, H)])
    ix = np.concatenate([middle_h, middle_l], 0)
    tables = [jnp.asarray(v) for v in (f_h, f_l, ft_h, ft_l, it_h, it_l, ix, iy, fy_hh)]

    mine = jnp.concatenate([mask_init, target_map.astype(jnp.float32)], 0)
    mate = lax.ppermute(mine, "gy", swap)
    own = jnp.where(
        core == 0, jnp.concatenate([mine, mate], 1), jnp.concatenate([mate, mine], 1)
    )
    far = jnp.concatenate([own[:H], jnp.where(core == 0, own[H + R :], own[H : H + R])], 0)
    s1 = lax.ppermute(own, ("gx", "gy"), ring(1))
    s2 = lax.ppermute(far, ("gx", "gy"), ring(2))
    r1 = lax.ppermute(s1, "gy", swap)
    r2 = lax.ppermute(s2, "gy", swap)

    where = jnp.stack([core, tile, jnp.int32(tiles * H)]).astype(jnp.int32)
    params = pltpu.CompilerParams(vmem_limit_bytes=56 << 20)
    rest, send, target = pl.pallas_call(
        first_kernel,
        out_shape=(shape(3 * H, N), shape(3 * H, H), shape(2 * H, H)),
        in_specs=[SMEM] + [VMEM] * (7 + len(tables)),
        out_specs=(VMEM,) * 3,
        scratch_shapes=scratch(4, 3, count),
        compiler_params=params,
        name="first_step",
    )(where, own, s1, r1, s2, r2, p, q, *tables)
    got = lax.ppermute(send, "gy", swap)
    mask, send, resist = pl.pallas_call(
        second_kernel,
        out_shape=(shape(H, H), shape(H, H), shape(H, H)),
        in_specs=[SMEM] + [VMEM] * (5 + len(tables)),
        out_specs=(VMEM,) * 3,
        scratch_shapes=scratch(2, 1, count),
        compiler_params=params,
        name="second_step",
    )(where, rest, got, target, p, q, *tables)
    return mask - lax.ppermute(send, "gy", swap), resist


def solution(mesh):
    spec = P(("win", "gx"), "gy")
    return jax.shard_map(
        functools.partial(per_device, tiles=mesh.shape["gx"]),
        mesh=mesh,
        in_specs=(spec, spec, P()),
        out_specs=(spec, spec),
        check_vma=False,
    )
```

```python
import functools

import jax
import jax.numpy as jnp
import ml_dtypes
import numpy as np
from jax import lax
from jax.experimental import pallas as pl
from jax.experimental.pallas import tpu as pltpu
from jax.sharding import PartitionSpec as P

STEP = 0.1
STEEP = 4.0
THRESHOLD = 1.5
N = 256
H = 128
R = 64
VMEM = pl.BlockSpec(memory_space=pltpu.VMEM)


def stack(table, axis):
    high = table.astype(ml_dtypes.bfloat16)
    low = (table - high.astype(np.float64)).astype(ml_dtypes.bfloat16)
    return np.concatenate([high, low, high], axis)


def wave_tables():
    place = np.arange(N)
    freq = np.arange(H)
    angle = 2.0 * np.pi * ((freq[:, None] * place[None, :]) % N) / N
    forward = np.concatenate([np.cos(angle), np.sin(angle)], 0)
    forward[H] = np.where(place % 2 == 0, 1.0, -1.0)
    weight = np.full((N,), 2.0)
    weight[0] = weight[H] = 1.0
    inverse = (forward * weight[:, None] / N).T
    return forward, inverse


def spectrum_tables(size, rows):
    slot = np.arange(N)
    freq = np.where(slot < H, slot, np.where(slot == H, H, slot - H))
    b = np.arange(size) - (size - 1) // 2
    right = np.zeros((N, N + H))
    right[:size, :N] = np.cos(2.0 * np.pi * ((b[:, None] * freq[None, :]) % N) / N)
    right[:size, N:] = np.sin(2.0 * np.pi * ((b[:, None] * slot[None, :H]) % N) / N)
    a = np.arange((size + 1) // 2)
    fold = np.where(a == 0, 1.0, 2.0)
    left_cos = np.zeros((N, rows))
    left_cos[:, : a.size] = fold * np.cos(2.0 * np.pi * ((freq[:, None] * a[None, :]) % N) / N)
    left_sin = np.zeros((H, rows))
    left_sin[:, : a.size] = fold * np.sin(2.0 * np.pi * ((slot[:H, None] * a[None, :]) % N) / N)
    return right, left_cos, left_sin


def split(value):
    high = value.astype(jnp.bfloat16)
    low = (value - high.astype(jnp.float32)).astype(jnp.bfloat16)
    return high, low


def dot(left, right):
    return jnp.dot(left, right, preferred_element_type=jnp.float32)


def left(table, value):
    high, low = value
    return dot(table, jnp.concatenate([high, high, low], 0))


def right(value, table):
    high, low = value
    return dot(jnp.concatenate([high, high, low], 1), table)


def mix(f, p_ref, q_ref, k):
    q = q_ref[k]
    cc, cs, sc, ss = f[:H, :H], f[:H, H:], f[H:, :H], f[H:, H:]
    return jnp.concatenate(
        [
            jnp.concatenate(
                [p_ref[k, :H, :H] * cc + q * ss, p_ref[k, :H, H:] * cs - q * sc], 1
            ),
            jnp.concatenate(
                [p_ref[k, H:, :H] * sc - q * cs, p_ref[k, H:, H:] * ss + q * cc], 1
            ),
        ],
        0,
    )


def amplitudes(blocks, field, p_ref, q_ref, t, f_sc, a_sc, core):
    ey = split(right(split(field), t["fy"][...]))
    for b in range(blocks):
        rows = slice(b * H, b * H + N)
        f_sc[b] = left(t["fx"][...], (ey[0][rows], ey[1][rows]))
    for k in range(p_ref.shape[0]):
        for b in range(blocks):
            x = left(t["ix"][...], split(mix(f_sc[b], p_ref, q_ref, k)))
            a_sc[k, b * H : (b + 1) * H, :] = right(split(x), t["iy_own"][core])


def slopes(rows, count, a_sc, target, inside, w_sc):
    total = a_sc[0, :rows, :] * a_sc[0, :rows, :]
    for k in range(1, count):
        total = total + a_sc[k, :rows, :] * a_sc[k, :rows, :]
    resist = 1.0 / (1.0 + jnp.exp(-STEEP * (total - THRESHOLD)))
    slope = 2.0 * (resist - target) * STEEP * resist * (1.0 - resist)
    slope = jnp.where(inside, 2.0 * slope, 0.0)
    for k in range(count):
        high, low = split(a_sc[k, :rows, :] * slope)
        w_sc[k, :rows, :H] = high
        w_sc[k, :rows, H:] = low
    return resist


def gradients(blocks, p_ref, q_ref, t, w_sc, z_sc, core):
    rows = (blocks + 1) * H
    for k in range(p_ref.shape[0]):
        w = w_sc[k, :rows, :]
        high, low = split(dot(jnp.concatenate([w, w[:, :H]], 1), t["fy_own"][core]))
        for b in range(blocks):
            part = slice(b * H, b * H + N)
            z = mix(left(t["fx"][...], (high[part], low[part])), p_ref, q_ref, k)
            z_sc[b] = z if k == 0 else z_sc[b] + z
    return [
        right(split(left(t["ix"][...], split(z_sc[b]))), t["iy"][...]) for b in range(blocks)
    ]


def lane_mask(shape, core):
    lane = lax.broadcasted_iota(jnp.int32, shape, 1)
    return (lane >= core * R) & (lane < N - R + core * R)


def row_mask(shape, first, total):
    row = lax.broadcasted_iota(jnp.int32, shape, 0) + first
    return (row >= 0) & (row < total)


def spectrum_kernel(k_ref, right_ref, cos_ref, sin_ref, p_ref, q_ref):
    count = p_ref.shape[0]
    rows = k_ref.shape[0] // count
    section = right(split(k_ref[...]), right_ref[...])
    for k in range(count):
        high, low = split(section[k * rows : (k + 1) * rows])
        p_ref[k] = left(cos_ref[...], (high[:, :N], low[:, :N]))
        q_ref[k] = left(sin_ref[...], (high[:, N:], low[:, N:]))


TABLES = ("fx", "fy", "fy_own", "ix", "iy", "iy_own")


def first_kernel(tiles, own_ref, s1_ref, r1_ref, s2_ref, r2_ref, p_ref, q_ref, *refs):
    t = dict(zip(TABLES, refs))
    rest_ref, send_ref, target_ref, f_sc, a_sc, w_sc, z_sc = refs[len(TABLES) :]
    core, tile, total = lax.axis_index("gy"), lax.axis_index("gx"), tiles * H
    count = p_ref.shape[0]
    low1 = jnp.where(core == 0, s1_ref[...], r1_ref[...])
    upp1 = jnp.where(core == 0, r1_ref[...], s1_ref[...])
    low2 = jnp.where(core == 0, s2_ref[...], r2_ref[...])
    upp2 = jnp.where(core == 0, r2_ref[...], s2_ref[...])
    field = jnp.concatenate([low2[:H], low1[:H], own_ref[:H], upp1[:H], upp2[:H]], 0)
    inside = row_mask(field.shape, (tile - 2) * H, total) & lane_mask(field.shape, core)
    field = jnp.where(inside, field, 0.0)
    target = jnp.concatenate([low2[H:], low1[H:], own_ref[H:], upp1[H:], upp2[H:]], 0)
    target = jnp.where(core == 0, target[:, :H], target[:, H:])
    amplitudes(4, field, p_ref, q_ref, t, f_sc, a_sc, core)
    slopes(4 * H, count, a_sc, target, row_mask((4 * H, H), (tile - 1) * H - R, total), w_sc)
    target_ref[...] = target[H : 3 * H]
    for b, part in enumerate(gradients(3, p_ref, q_ref, t, w_sc, z_sc, core)):
        rows = slice(b * H, (b + 1) * H)
        rest_ref[rows, :] = field[(b + 1) * H : (b + 2) * H] - STEP * part
        send_ref[rows, :] = pltpu.roll(part, N - R, 1)[:, :H]


def second_kernel(tiles, rest_ref, got_ref, target_ref, p_ref, q_ref, *refs):
    t = dict(zip(TABLES, refs))
    mask_ref, send_ref, resist_ref, f_sc, a_sc, w_sc, z_sc = refs[len(TABLES) :]
    core, tile, total = lax.axis_index("gy"), lax.axis_index("gx"), tiles * H
    count = p_ref.shape[0]
    got = jnp.concatenate([got_ref[...], jnp.zeros_like(got_ref)], 1)
    field = rest_ref[...] - STEP * pltpu.roll(got, R, 1)
    inside = row_mask(field.shape, (tile - 1) * H, total) & lane_mask(field.shape, core)
    field = jnp.where(inside, field, 0.0)
    amplitudes(2, field, p_ref, q_ref, t, f_sc, a_sc, core)
    inside = row_mask((2 * H, H), tile * H - R, total)
    resist = slopes(2 * H, count, a_sc, target_ref[...], inside, w_sc)
    resist_ref[...] = resist[R : R + H]
    (part,) = gradients(1, p_ref, q_ref, t, w_sc, z_sc, core)
    part = jnp.where(lane_mask(part.shape, core), STEP * part, 0.0)
    own = field[H : 2 * H] - part
    mask_ref[...] = jnp.where(core == 0, own[:, :H], own[:, H:])
    send_ref[...] = jnp.where(core == 0, part[:, H:], part[:, :H])


def shape(*dims, dtype=jnp.float32):
    return jax.ShapeDtypeStruct(dims, dtype)


def scratch(blocks, adjoint_blocks, count):
    return [
        pltpu.VMEM((blocks, N, N), jnp.float32),
        pltpu.VMEM((count, blocks * H, H), jnp.float32),
        pltpu.VMEM((count, blocks * H, N), jnp.bfloat16),
        pltpu.VMEM((adjoint_blocks, N, N), jnp.float32),
    ]


def per_device(mask_init, target_map, kernels, tiles):
    count, size, _ = kernels.shape
    core = lax.axis_index("gy")
    tile = lax.axis_index("gx")
    swap = [(0, 1), (1, 0)]

    def place(step):
        step %= 2 * tiles
        return 2 * step if step < tiles else 2 * (2 * tiles - 1 - step) + 1

    def ring(shift):
        return [(place(i), place(i + shift)) for i in range(2 * tiles)]

    rows = 72
    half = jnp.pad(
        kernels[:, (size - 1) // 2 :, :],
        ((0, 0), (0, rows - (size + 1) // 2), (0, N - size)),
    ).reshape(count * rows, N)
    right_table, left_cos, left_sin = spectrum_tables(size, rows)
    spectral = [stack(right_table, 0), stack(left_cos, 1), stack(left_sin, 1)]
    spectral = [jnp.asarray(v) for v in spectral]
    p, q = pl.pallas_call(
        spectrum_kernel,
        out_shape=(shape(count, N, N), shape(count, H, H)),
        in_specs=[VMEM] * 4,
        out_specs=(VMEM, VMEM),
        cost_estimate=pl.CostEstimate(
            flops=6 * count * rows * N * N * 4, bytes_accessed=4 * count * N * N, transcendentals=0
        ),
        compiler_params=pltpu.CompilerParams(vmem_limit_bytes=12 << 20),
        name="spectra",
    )(half, *spectral)

    forward, inverse = wave_tables()
    halves = [slice(c, c + H) for c in (0, H)]
    tables = [
        stack(forward, 1),
        stack(forward.T, 0),
        np.stack([np.roll(stack(forward.T[c], 0), H, 0) for c in halves]),
        stack(inverse[R : R + H], 1),
        stack(inverse.T, 0),
        np.stack([stack(inverse.T[:, c], 0) for c in halves]),
    ]
    tables = [jnp.asarray(v) for v in tables]

    mine = jnp.concatenate([mask_init, target_map.astype(jnp.float32)], 0)
    mate = lax.ppermute(mine, "gy", swap)
    own = jnp.where(
        core == 0, jnp.concatenate([mine, mate], 1), jnp.concatenate([mate, mine], 1)
    )
    far = jnp.concatenate([own[:H], jnp.where(core == 0, own[H + R :], own[H : H + R])], 0)
    s1 = lax.ppermute(own, ("gx", "gy"), ring(1))
    s2 = lax.ppermute(far, ("gx", "gy"), ring(2))
    r1 = lax.ppermute(s1, "gy", swap)
    r2 = lax.ppermute(s2, "gy", swap)

    params = pltpu.CompilerParams(vmem_limit_bytes=40 << 20)
    rest, send, target = pl.pallas_call(
        functools.partial(first_kernel, tiles),
        out_shape=(shape(3 * H, N), shape(3 * H, H), shape(2 * H, H)),
        in_specs=[VMEM] * (7 + len(tables)),
        out_specs=(VMEM,) * 3,
        scratch_shapes=scratch(4, 3, count),
        compiler_params=params,
        name="first_step",
    )(own, s1, r1, s2, r2, p, q, *tables)
    got = lax.ppermute(send, "gy", swap)
    mask, send, resist = pl.pallas_call(
        functools.partial(second_kernel, tiles),
        out_shape=(shape(H, H), shape(H, H), shape(H, H)),
        in_specs=[VMEM] * (5 + len(tables)),
        out_specs=(VMEM,) * 3,
        scratch_shapes=scratch(2, 1, count),
        compiler_params=params,
        name="second_step",
    )(rest, got, target, p, q, *tables)
    return mask - lax.ppermute(send, "gy", swap), resist


def solution(mesh):
    spec = P(("win", "gx"), "gy")
    return jax.shard_map(
        functools.partial(per_device, tiles=mesh.shape["gx"]),
        mesh=mesh,
        in_specs=(spec, spec, P()),
        out_specs=(spec, spec),
        check_vma=False,
    )
```

```python
import functools

import jax
import jax.numpy as jnp
import ml_dtypes
import numpy as np
from jax import lax
from jax.experimental import pallas as pl
from jax.experimental.pallas import tpu as pltpu
from jax.sharding import PartitionSpec as P

STEP = 0.1
STEEP = 4.0
THRESHOLD = 1.5
N = 256
H = 128
R = 64
VMEM = pl.BlockSpec(memory_space=pltpu.VMEM)


def stack(table, axis):
    high = table.astype(ml_dtypes.bfloat16)
    low = (table - high.astype(np.float64)).astype(ml_dtypes.bfloat16)
    return np.concatenate([high, low, high], axis)


def waves(freqs, places):
    angle = np.pi / N * ((2 * freqs + 1) * places % (2 * N))
    return np.cos(angle), np.sin(angle)


def wave_tables():
    forward = np.concatenate(waves(np.arange(H)[:, None], np.arange(N)[None, :]), 0)
    return forward, forward.T * (2.0 / N)


def spectrum_tables(size, rows):
    freq = np.arange(H)
    places = np.arange(size) - (size - 1) // 2
    right = np.zeros((N, N))
    right[:size] = np.concatenate(waves(freq[None, :], places[:, None]), 1)
    below = np.arange((size + 1) // 2)
    left = np.zeros((2, H, rows))
    left[:, :, : below.size] = waves(freq[:, None], below[None, :])
    left[:, :, 1:] *= 2.0
    return right, left[0], left[1]


def split(value):
    high = value.astype(jnp.bfloat16)
    low = (value - high.astype(jnp.float32)).astype(jnp.bfloat16)
    return high, low


def dot(left, right):
    return jnp.dot(left, right, preferred_element_type=jnp.float32)


def left(table, value):
    high, low = value
    return dot(table, jnp.concatenate([high, high, low], 0))


def right(value, table):
    high, low = value
    return dot(jnp.concatenate([high, high, low], 1), table)


def mix(f, p, q, rows):
    upper = slice(rows.start, rows.stop)
    lower = slice(H + rows.start, H + rows.stop)
    cc, cs, sc, ss = f[upper, :H], f[upper, H:], f[lower, :H], f[lower, H:]
    p, q = p[rows], q[rows]
    return p * cc + q * ss, p * cs - q * sc, p * sc - q * cs, p * ss + q * cc


def store_quarters(ref, rows, quarters):
    lower = slice(H + rows.start, H + rows.stop)
    places = ((rows, slice(0, H)), (rows, slice(H, N)), (lower, slice(0, H)), (lower, slice(H, N)))
    for (x, y), quarter in zip(places, quarters):
        ref[0, x, y], ref[1, x, y] = split(quarter)


CHUNKS = [slice(r, r + 16) for r in range(0, H, 16)]


def pipeline(count, *stages):
    for step in range(count + len(stages) - 1):
        for lag, stage in enumerate(reversed(stages)):
            item = step - (len(stages) - 1 - lag)
            if 0 <= item < count:
                stage(item)


def amplitudes(blocks, field, p_ref, q_ref, t, f_sc, g_sc, x_sc, a_sc, core):
    ey = split(right(split(field), t["fy"][...]))
    for b in range(blocks):
        rows = slice(b * H, b * H + N)
        f_sc[b] = left(t["fx"][...], (ey[0][rows], ey[1][rows]))

    def mixed(i):
        k, b = i // blocks, i % blocks
        for rows in CHUNKS:
            quarters = mix(f_sc.at[b], p_ref.at[k], q_ref.at[k], rows)
            store_quarters(g_sc.at[i], rows, quarters)

    def inverse_x(i):
        x = left(t["ix"][...], (g_sc[i, 0], g_sc[i, 1]))
        x_sc[0, i], x_sc[1, i] = split(x)

    def inverse_y(i):
        k, b = i // blocks, i % blocks
        a_sc[k, b * H : (b + 1) * H, :] = right((x_sc[0, i], x_sc[1, i]), t["iy_own"][core])

    pipeline(p_ref.shape[0] * blocks, mixed, inverse_x, inverse_y)


def slopes(blocks, count, a_sc, target, inside, w_sc):
    resists = []
    for c in range(0, blocks * H, R):
        rows = slice(c, c + R)
        amplitude = [a_sc[k, rows, :] for k in range(count)]
        total = amplitude[0] * amplitude[0]
        for k in range(1, count):
            total = total + amplitude[k] * amplitude[k]
        resist = 1.0 / (1.0 + jnp.exp(-STEEP * (total - THRESHOLD)))
        slope = 2.0 * (resist - target[rows]) * STEEP * resist * (1.0 - resist)
        slope = jnp.where(inside[rows], 2.0 * slope, 0.0)
        for k in range(count):
            cols = slice(k * H, (k + 1) * H)
            w_sc[0, rows, cols], w_sc[1, rows, cols] = split(amplitude[k] * slope)
        resists.append(resist)
    return resists


def gradients(blocks, count, p_ref, q_ref, t, w_sc, y_sc, u_sc, z_sc, core):
    def forward_x(b):
        rows = slice(b * H, b * H + N)
        y = left(t["fx"][...], (w_sc[0, rows, :], w_sc[1, rows, :]))
        y_sc[0, b], y_sc[1, b] = split(y)

    def forward_y(b):
        for k in range(count):
            cols = slice(k * H, (k + 1) * H)
            u_sc[b, k] = right((y_sc[0, b, :, cols], y_sc[1, b, :, cols]), t["fy_own"][core])

    def mixed(b):
        for rows in CHUNKS:
            terms = [mix(u_sc.at[b, k], p_ref.at[k], q_ref.at[k], rows) for k in range(count)]
            store_quarters(z_sc.at[b], rows, [sum(quarter) for quarter in zip(*terms)])

    def inverse_x(b):
        y_sc[0, b, :H, :N], y_sc[1, b, :H, :N] = split(left(t["ix"][...], (z_sc[b, 0], z_sc[b, 1])))

    out = []

    def inverse_y(b):
        out.append(right((y_sc[0, b, :H, :N], y_sc[1, b, :H, :N]), t["iy"][...]))

    pipeline(blocks, forward_x, forward_y, mixed, inverse_x, inverse_y)
    return out


def lane_mask(shape, core):
    lane = lax.broadcasted_iota(jnp.int32, shape, 1)
    return (lane >= core * R) & (lane < N - R + core * R)


def row_mask(shape, first, total):
    row = lax.broadcasted_iota(jnp.int32, shape, 0) + first
    return (row >= 0) & (row < total)


def spectrum_kernel(k_ref, right_ref, cos_ref, sin_ref, p_ref, q_ref):
    count = p_ref.shape[0]
    rows = k_ref.shape[0] // count
    section = right(split(k_ref[...]), right_ref[...])
    for k in range(count):
        high, low = split(section[k * rows : (k + 1) * rows])
        p_ref[k] = left(cos_ref[...], (high[:, :H], low[:, :H]))
        q_ref[k] = left(sin_ref[...], (high[:, H:], low[:, H:]))


TABLES = ("fx", "fy", "fy_own", "ix", "iy", "iy_own")


def first_kernel(tiles, own_ref, s1_ref, r1_ref, s2_ref, r2_ref, p_ref, q_ref, *refs):
    t = dict(zip(TABLES, refs))
    rest_ref, send_ref, target_ref, f_sc, g_sc, x_sc, a_sc, w_sc, y_sc, u_sc, z_sc = refs[len(TABLES) :]
    core, tile, total = lax.axis_index("gy"), lax.axis_index("gx"), tiles * H
    count = p_ref.shape[0]
    low1 = jnp.where(core == 0, s1_ref[...], r1_ref[...])
    upp1 = jnp.where(core == 0, r1_ref[...], s1_ref[...])
    low2 = jnp.where(core == 0, s2_ref[...], r2_ref[...])
    upp2 = jnp.where(core == 0, r2_ref[...], s2_ref[...])
    field = jnp.concatenate([low2[:H], low1[:H], own_ref[:H], upp1[:H], upp2[:H]], 0)
    inside = row_mask(field.shape, (tile - 2) * H, total) & lane_mask(field.shape, core)
    field = jnp.where(inside, field, 0.0)
    target = jnp.concatenate([low2[H:], low1[H:], own_ref[H:], upp1[H:], upp2[H:]], 0)
    target = jnp.where(core == 0, target[:, :H], target[:, H:])
    amplitudes(4, field, p_ref, q_ref, t, f_sc, g_sc, x_sc, a_sc, core)
    slopes(4, count, a_sc, target, row_mask((4 * H, H), (tile - 1) * H - R, total), w_sc)
    target_ref[...] = target[H : 3 * H]
    for b, part in enumerate(gradients(3, count, p_ref, q_ref, t, w_sc, y_sc, u_sc, z_sc, core)):
        rows = slice(b * H, (b + 1) * H)
        rest_ref[rows, :] = field[(b + 1) * H : (b + 2) * H] - STEP * part
        send_ref[rows, :] = pltpu.roll(part, N - R, 1)[:, :H]


def second_kernel(tiles, rest_ref, got_ref, target_ref, p_ref, q_ref, *refs):
    t = dict(zip(TABLES, refs))
    mask_ref, send_ref, resist_ref, f_sc, g_sc, x_sc, a_sc, w_sc, y_sc, u_sc, z_sc = refs[len(TABLES) :]
    core, tile, total = lax.axis_index("gy"), lax.axis_index("gx"), tiles * H
    count = p_ref.shape[0]
    got = jnp.concatenate([got_ref[...], jnp.zeros_like(got_ref)], 1)
    field = rest_ref[...] - STEP * pltpu.roll(got, R, 1)
    inside = row_mask(field.shape, (tile - 1) * H, total) & lane_mask(field.shape, core)
    field = jnp.where(inside, field, 0.0)
    amplitudes(2, field, p_ref, q_ref, t, f_sc, g_sc, x_sc, a_sc, core)
    inside = row_mask((2 * H, H), tile * H - R, total)
    resist = slopes(2, count, a_sc, target_ref[...], inside, w_sc)
    resist_ref[:R, :], resist_ref[R:, :] = resist[1], resist[2]
    (part,) = gradients(1, count, p_ref, q_ref, t, w_sc, y_sc, u_sc, z_sc, core)
    part = jnp.where(lane_mask(part.shape, core), STEP * part, 0.0)
    own = field[H : 2 * H] - part
    mask_ref[...] = jnp.where(core == 0, own[:, :H], own[:, H:])
    send_ref[...] = jnp.where(core == 0, part[:, H:], part[:, :H])


def shape(*dims, dtype=jnp.float32):
    return jax.ShapeDtypeStruct(dims, dtype)


def scratch(blocks, adjoint_blocks, count):
    items = count * blocks
    return [
        pltpu.VMEM((blocks, N, N), jnp.float32),
        pltpu.VMEM((items, 2, N, N), jnp.bfloat16),
        pltpu.VMEM((2, items, H, N), jnp.bfloat16),
        pltpu.VMEM((count, blocks * H, H), jnp.float32),
        pltpu.VMEM((2, blocks * H, count * H), jnp.bfloat16),
        pltpu.VMEM((2, adjoint_blocks, N, count * H), jnp.bfloat16),
        pltpu.VMEM((adjoint_blocks, count, N, N), jnp.float32),
        pltpu.VMEM((adjoint_blocks, 2, N, N), jnp.bfloat16),
    ]


def per_device(mask_init, target_map, kernels, tiles):
    count, size, _ = kernels.shape
    core = lax.axis_index("gy")
    tile = lax.axis_index("gx")
    swap = [(0, 1), (1, 0)]

    def place(step):
        step %= 2 * tiles
        return 2 * step if step < tiles else 2 * (2 * tiles - 1 - step) + 1

    def ring(shift):
        return [(place(i), place(i + shift)) for i in range(2 * tiles)]

    rows = 72
    half = jnp.pad(
        kernels[:, (size - 1) // 2 :, :],
        ((0, 0), (0, rows - (size + 1) // 2), (0, N - size)),
    ).reshape(count * rows, N)
    right_table, left_cos, left_sin = spectrum_tables(size, rows)
    spectral = [stack(right_table, 0), stack(left_cos, 1), stack(left_sin, 1)]
    spectral = [jnp.asarray(v) for v in spectral]
    p, q = pl.pallas_call(
        spectrum_kernel,
        out_shape=(shape(count, H, H), shape(count, H, H)),
        in_specs=[VMEM] * 4,
        out_specs=(VMEM, VMEM),
        cost_estimate=pl.CostEstimate(
            flops=6 * count * rows * N * N * 4, bytes_accessed=4 * count * N * N, transcendentals=0
        ),
        compiler_params=pltpu.CompilerParams(vmem_limit_bytes=12 << 20),
        name="spectra",
    )(half, *spectral)

    forward, inverse = wave_tables()
    halves = [slice(c, c + H) for c in (0, H)]
    tables = [
        stack(forward, 1),
        stack(forward.T, 0),
        np.stack([stack(forward.T[c], 0) for c in halves]),
        stack(inverse[R : R + H], 1),
        stack(inverse.T, 0),
        np.stack([stack(inverse.T[:, c], 0) for c in halves]),
    ]
    tables = [jnp.asarray(v) for v in tables]

    mine = jnp.concatenate([mask_init, target_map.astype(jnp.float32)], 0)
    mate = lax.ppermute(mine, "gy", swap)
    own = jnp.where(
        core == 0, jnp.concatenate([mine, mate], 1), jnp.concatenate([mate, mine], 1)
    )
    far = jnp.concatenate([own[:H], jnp.where(core == 0, own[H + R :], own[H : H + R])], 0)
    s1 = lax.ppermute(own, ("gx", "gy"), ring(1))
    s2 = lax.ppermute(far, ("gx", "gy"), ring(2))
    r1 = lax.ppermute(s1, "gy", swap)
    r2 = lax.ppermute(s2, "gy", swap)

    params = pltpu.CompilerParams(vmem_limit_bytes=40 << 20)
    rest, send, target = pl.pallas_call(
        functools.partial(first_kernel, tiles),
        out_shape=(shape(3 * H, N), shape(3 * H, H), shape(2 * H, H)),
        in_specs=[VMEM] * (7 + len(tables)),
        out_specs=(VMEM,) * 3,
        scratch_shapes=scratch(4, 3, count),
        compiler_params=params,
        name="first_step",
    )(own, s1, r1, s2, r2, p, q, *tables)
    got = lax.ppermute(send, "gy", swap)
    mask, send, resist = pl.pallas_call(
        functools.partial(second_kernel, tiles),
        out_shape=(shape(H, H), shape(H, H), shape(H, H)),
        in_specs=[VMEM] * (5 + len(tables)),
        out_specs=(VMEM,) * 3,
        scratch_shapes=scratch(2, 1, count),
        compiler_params=params,
        name="second_step",
    )(rest, got, target, p, q, *tables)
    return mask - lax.ppermute(send, "gy", swap), resist


def solution(mesh):
    spec = P(("win", "gx"), "gy")
    return jax.shard_map(
        functools.partial(per_device, tiles=mesh.shape["gx"]),
        mesh=mesh,
        in_specs=(spec, spec, P()),
        out_specs=(spec, spec),
        check_vma=False,
    )
```

```python
import functools

import jax
import jax.numpy as jnp
import ml_dtypes
import numpy as np
from jax import lax
from jax.experimental import pallas as pl
from jax.experimental.pallas import tpu as pltpu
from jax.sharding import PartitionSpec as P

STEP = 0.1
STEEP = 4.0
THRESHOLD = 1.5
N = 256
H = 128
R = 64
VMEM = pl.BlockSpec(memory_space=pltpu.VMEM)


def stack(table, axis):
    high = table.astype(ml_dtypes.bfloat16)
    low = (table - high.astype(np.float64)).astype(ml_dtypes.bfloat16)
    return np.concatenate([high, low, high], axis)


def waves(freqs, places):
    angle = np.pi / N * ((2 * freqs + 1) * places % (2 * N))
    return np.cos(angle), np.sin(angle)


def wave_tables():
    forward = np.concatenate(waves(np.arange(H)[:, None], np.arange(N)[None, :]), 0)
    return forward, forward.T * (2.0 / N)


def spectrum_tables(size, rows):
    freq = np.arange(H)
    places = np.arange(size) - (size - 1) // 2
    right = np.zeros((N, N))
    right[:size] = np.concatenate(waves(freq[None, :], places[:, None]), 1)
    below = np.arange((size + 1) // 2)
    left = np.zeros((2, H, rows))
    left[:, :, : below.size] = waves(freq[:, None], below[None, :])
    left[:, :, 1:] *= 2.0
    return right, left[0], left[1]


def split(value):
    high = value.astype(jnp.bfloat16)
    low = (value - high.astype(jnp.float32)).astype(jnp.bfloat16)
    return high, low


def dot(left, right):
    return jnp.dot(left, right, preferred_element_type=jnp.float32)


def left(table, value):
    high, low = value
    return dot(table, jnp.concatenate([high, high, low], 0))


def right(value, table):
    high, low = value
    return dot(jnp.concatenate([high, high, low], 1), table)


def mix(f, p, q, rows):
    upper = slice(rows.start, rows.stop)
    lower = slice(H + rows.start, H + rows.stop)
    cc, cs, sc, ss = f[upper, :H], f[upper, H:], f[lower, :H], f[lower, H:]
    p, q = p[rows], q[rows]
    return p * cc + q * ss, p * cs - q * sc, p * sc - q * cs, p * ss + q * cc


def store_quarters(ref, rows, quarters):
    lower = slice(H + rows.start, H + rows.stop)
    places = ((rows, slice(0, H)), (rows, slice(H, N)), (lower, slice(0, H)), (lower, slice(H, N)))
    for (x, y), quarter in zip(places, quarters):
        ref[0, x, y], ref[1, x, y] = split(quarter)


CHUNKS = [slice(r, r + 16) for r in range(0, H, 16)]


def pipeline(count, *stages):
    for step in range(count + len(stages) - 1):
        for lag, stage in enumerate(reversed(stages)):
            item = step - (len(stages) - 1 - lag)
            if 0 <= item < count:
                stage(item)


def amplitudes(blocks, field, p_ref, q_ref, t, f_sc, g_sc, x_sc, a_sc, core):
    ey = split(right(split(field), t["fy"][...]))
    for b in range(blocks):
        rows = slice(b * H, b * H + N)
        f_sc[b] = left(t["fx"][...], (ey[0][rows], ey[1][rows]))

    def mixed(i):
        k, b = i // blocks, i % blocks
        for rows in CHUNKS:
            quarters = mix(f_sc.at[b], p_ref.at[k], q_ref.at[k], rows)
            store_quarters(g_sc.at[i], rows, quarters)

    def inverse_x(i):
        x = left(t["ix"][...], (g_sc[i, 0], g_sc[i, 1]))
        x_sc[0, i], x_sc[1, i] = split(x)

    def inverse_y(i):
        k, b = i // blocks, i % blocks
        a_sc[k, b * H : (b + 1) * H, :] = right((x_sc[0, i], x_sc[1, i]), t["iy_own"][core])

    pipeline(p_ref.shape[0] * blocks, mixed, inverse_x, inverse_y)


def slopes(blocks, count, a_sc, target, inside, w_sc):
    resists = []
    for c in range(0, blocks * H, R):
        rows = slice(c, c + R)
        amplitude = [a_sc[k, rows, :] for k in range(count)]
        total = amplitude[0] * amplitude[0]
        for k in range(1, count):
            total = total + amplitude[k] * amplitude[k]
        resist = 1.0 / (1.0 + jnp.exp(-STEEP * (total - THRESHOLD)))
        slope = 2.0 * (resist - target[rows]) * STEEP * resist * (1.0 - resist)
        slope = jnp.where(inside[rows], 2.0 * slope, 0.0)
        for k in range(count):
            cols = slice(k * H, (k + 1) * H)
            w_sc[0, rows, cols], w_sc[1, rows, cols] = split(amplitude[k] * slope)
        resists.append(resist)
    return resists


def gradients(blocks, count, p_ref, q_ref, t, w_sc, y_sc, u_sc, z_sc, core):
    def forward_x(b):
        rows = slice(b * H, b * H + N)
        y = left(t["fx"][...], (w_sc[0, rows, :], w_sc[1, rows, :]))
        y_sc[0, b], y_sc[1, b] = split(y)

    def forward_y(b):
        for k in range(count):
            cols = slice(k * H, (k + 1) * H)
            u_sc[b, k] = right((y_sc[0, b, :, cols], y_sc[1, b, :, cols]), t["fy_own"][core])

    def mixed(b):
        for rows in CHUNKS:
            terms = [mix(u_sc.at[b, k], p_ref.at[k], q_ref.at[k], rows) for k in range(count)]
            store_quarters(z_sc.at[b], rows, [sum(quarter) for quarter in zip(*terms)])

    def inverse_x(b):
        y_sc[0, b, :H, :N], y_sc[1, b, :H, :N] = split(left(t["ix"][...], (z_sc[b, 0], z_sc[b, 1])))

    out = []

    def inverse_y(b):
        out.append(right((y_sc[0, b, :H, :N], y_sc[1, b, :H, :N]), t["iy"][...]))

    pipeline(blocks, forward_x, forward_y, mixed, inverse_x, inverse_y)
    return out


def lane_mask(shape, core):
    lane = lax.broadcasted_iota(jnp.int32, shape, 1)
    return (lane >= core * R) & (lane < N - R + core * R)


def row_mask(shape, first, total):
    row = lax.broadcasted_iota(jnp.int32, shape, 0) + first
    return (row >= 0) & (row < total)


def spectrum_kernel(k_ref, right_ref, cos_ref, sin_ref, p_ref, q_ref):
    count = p_ref.shape[0]
    rows = k_ref.shape[0] // count
    section = right(split(k_ref[...]), right_ref[...])
    for k in range(count):
        high, low = split(section[k * rows : (k + 1) * rows])
        p_ref[k] = left(cos_ref[...], (high[:, :H], low[:, :H]))
        q_ref[k] = left(sin_ref[...], (high[:, H:], low[:, H:]))


TABLES = ("fx", "fy", "fy_own", "ix", "iy", "iy_own")


def first_kernel(tiles, near_ref, a1_ref, b1_ref, a2_ref, b2_ref, mate_ref, p_ref, q_ref, *refs):
    t = dict(zip(TABLES, refs))
    rest_ref, send_ref, target_ref, f_sc, g_sc, x_sc, a_sc, w_sc, y_sc, u_sc, z_sc = refs[len(TABLES) :]
    core, tile, total = lax.axis_index("gy"), lax.axis_index("gx"), tiles * H
    count = p_ref.shape[0]
    first = core == 0

    def ordered(*parts):
        pairs = zip(parts, parts[::-1])
        return jnp.concatenate([jnp.where(first, x, y) for x, y in pairs], 0)

    field = ordered(a2_ref[:H], a1_ref[:H], near_ref[:H], b1_ref[:H], b2_ref[:H])
    mate = [mate_ref[c * H : (c + 1) * H] for c in range(5)]
    mate = ordered(*mate[::-1])
    field = jnp.concatenate([jnp.where(first, field, mate), jnp.where(first, mate, field)], 1)
    inside = row_mask(field.shape, (tile - 2) * H, total) & lane_mask(field.shape, core)
    field = jnp.where(inside, field, 0.0)
    target = ordered(a2_ref[H:], a1_ref[H:], near_ref[H:], b1_ref[H:], b2_ref[H:])
    amplitudes(4, field, p_ref, q_ref, t, f_sc, g_sc, x_sc, a_sc, core)
    slopes(4, count, a_sc, target, row_mask((4 * H, H), (tile - 1) * H - R, total), w_sc)
    target_ref[...] = target[H : 3 * H]
    for b, part in enumerate(gradients(3, count, p_ref, q_ref, t, w_sc, y_sc, u_sc, z_sc, core)):
        rows = slice(b * H, (b + 1) * H)
        rest_ref[rows, :] = field[(b + 1) * H : (b + 2) * H] - STEP * part
        send_ref[rows, :] = pltpu.roll(part, N - R, 1)[:, :H]


def second_kernel(tiles, rest_ref, got_ref, target_ref, p_ref, q_ref, *refs):
    t = dict(zip(TABLES, refs))
    mask_ref, send_ref, resist_ref, f_sc, g_sc, x_sc, a_sc, w_sc, y_sc, u_sc, z_sc = refs[len(TABLES) :]
    core, tile, total = lax.axis_index("gy"), lax.axis_index("gx"), tiles * H
    count = p_ref.shape[0]
    got = jnp.concatenate([got_ref[...], jnp.zeros_like(got_ref)], 1)
    field = rest_ref[...] - STEP * pltpu.roll(got, R, 1)
    inside = row_mask(field.shape, (tile - 1) * H, total) & lane_mask(field.shape, core)
    field = jnp.where(inside, field, 0.0)
    amplitudes(2, field, p_ref, q_ref, t, f_sc, g_sc, x_sc, a_sc, core)
    inside = row_mask((2 * H, H), tile * H - R, total)
    resist = slopes(2, count, a_sc, target_ref[...], inside, w_sc)
    resist_ref[:R, :], resist_ref[R:, :] = resist[1], resist[2]
    (part,) = gradients(1, count, p_ref, q_ref, t, w_sc, y_sc, u_sc, z_sc, core)
    part = jnp.where(lane_mask(part.shape, core), STEP * part, 0.0)
    own = field[H : 2 * H] - part
    mask_ref[...] = jnp.where(core == 0, own[:, :H], own[:, H:])
    send_ref[...] = jnp.where(core == 0, part[:, H:], part[:, :H])


def shape(*dims, dtype=jnp.float32):
    return jax.ShapeDtypeStruct(dims, dtype)


def scratch(blocks, adjoint_blocks, count):
    items = count * blocks
    return [
        pltpu.VMEM((blocks, N, N), jnp.float32),
        pltpu.VMEM((items, 2, N, N), jnp.bfloat16),
        pltpu.VMEM((2, items, H, N), jnp.bfloat16),
        pltpu.VMEM((count, blocks * H, H), jnp.float32),
        pltpu.VMEM((2, blocks * H, count * H), jnp.bfloat16),
        pltpu.VMEM((2, adjoint_blocks, N, count * H), jnp.bfloat16),
        pltpu.VMEM((adjoint_blocks, count, N, N), jnp.float32),
        pltpu.VMEM((adjoint_blocks, 2, N, N), jnp.bfloat16),
    ]


def per_device(mask_init, target_map, kernels, tiles):
    count, size, _ = kernels.shape
    core = lax.axis_index("gy")
    tile = lax.axis_index("gx")
    swap = [(0, 1), (1, 0)]

    def place(step):
        step %= 2 * tiles
        return 2 * step if step < tiles else 2 * (2 * tiles - 1 - step) + 1

    def ring(shift):
        return [(place(i), place(i + shift)) for i in range(2 * tiles)]

    rows = 72
    half = jnp.pad(
        kernels[:, (size - 1) // 2 :, :],
        ((0, 0), (0, rows - (size + 1) // 2), (0, N - size)),
    ).reshape(count * rows, N)
    right_table, left_cos, left_sin = spectrum_tables(size, rows)
    spectral = [stack(right_table, 0), stack(left_cos, 1), stack(left_sin, 1)]
    spectral = [jnp.asarray(v) for v in spectral]
    p, q = pl.pallas_call(
        spectrum_kernel,
        out_shape=(shape(count, H, H), shape(count, H, H)),
        in_specs=[VMEM] * 4,
        out_specs=(VMEM, VMEM),
        cost_estimate=pl.CostEstimate(
            flops=6 * count * rows * N * N * 4, bytes_accessed=4 * count * N * N, transcendentals=0
        ),
        compiler_params=pltpu.CompilerParams(vmem_limit_bytes=12 << 20),
        name="spectra",
    )(half, *spectral)

    forward, inverse = wave_tables()
    halves = [slice(c, c + H) for c in (0, H)]
    tables = [
        stack(forward, 1),
        stack(forward.T, 0),
        np.stack([stack(forward.T[c], 0) for c in halves]),
        stack(inverse[R : R + H], 1),
        stack(inverse.T, 0),
        np.stack([stack(inverse.T[:, c], 0) for c in halves]),
    ]
    tables = [jnp.asarray(v) for v in tables]

    near = jnp.concatenate([mask_init, target_map.astype(jnp.float32)], 0)
    first, second = near[H : H + R], near[H + R :]
    up = jnp.concatenate([near[:H], jnp.where(core == 0, second, first)], 0)
    down = jnp.concatenate([near[:H], jnp.where(core == 0, first, second)], 0)
    both = ("gx", "gy")
    around = [
        lax.ppermute(near, both, ring(1)),
        lax.ppermute(near, both, ring(-1)),
        lax.ppermute(up, both, ring(2)),
        lax.ppermute(down, both, ring(-2)),
    ]
    *around, p, q = lax.optimization_barrier((*around, p, q))
    a1, b1, a2, b2 = around
    mate = lax.ppermute(
        jnp.concatenate([a2[:H], a1[:H], near[:H], b1[:H], b2[:H]], 0), "gy", swap
    )

    params = pltpu.CompilerParams(vmem_limit_bytes=40 << 20)
    rest, send, target = pl.pallas_call(
        functools.partial(first_kernel, tiles),
        out_shape=(shape(3 * H, N), shape(3 * H, H), shape(2 * H, H)),
        in_specs=[VMEM] * (8 + len(tables)),
        out_specs=(VMEM,) * 3,
        scratch_shapes=scratch(4, 3, count),
        compiler_params=params,
        name="first_step",
    )(near, a1, b1, a2, b2, mate, p, q, *tables)
    got = lax.ppermute(send, "gy", swap)
    mask, send, resist = pl.pallas_call(
        functools.partial(second_kernel, tiles),
        out_shape=(shape(H, H), shape(H, H), shape(H, H)),
        in_specs=[VMEM] * (5 + len(tables)),
        out_specs=(VMEM,) * 3,
        scratch_shapes=scratch(2, 1, count),
        compiler_params=params,
        name="second_step",
    )(rest, got, target, p, q, *tables)
    return mask - lax.ppermute(send, "gy", swap), resist


def solution(mesh):
    spec = P(("win", "gx"), "gy")
    return jax.shard_map(
        functools.partial(per_device, tiles=mesh.shape["gx"]),
        mesh=mesh,
        in_specs=(spec, spec, P()),
        out_specs=(spec, spec),
        check_vma=False,
    )
```

```python
import functools

import jax
import jax.numpy as jnp
import ml_dtypes
import numpy as np
from jax import lax
from jax.experimental import pallas as pl
from jax.experimental.pallas import tpu as pltpu
from jax.sharding import PartitionSpec as P

STEP = 0.1
STEEP = 4.0
THRESHOLD = 1.5
N = 256
H = 128
R = 64
VMEM = pl.BlockSpec(memory_space=pltpu.VMEM)


def stack(table, axis):
    high = table.astype(ml_dtypes.bfloat16)
    low = (table - high.astype(np.float64)).astype(ml_dtypes.bfloat16)
    return np.concatenate([high, low, high], axis)


def waves(freqs, places):
    angle = np.pi / N * ((2 * freqs + 1) * places % (2 * N))
    return np.cos(angle), np.sin(angle)


def wave_tables():
    forward = np.concatenate(waves(np.arange(H)[:, None], np.arange(N)[None, :]), 0)
    return forward, forward.T * (2.0 / N)


def spectrum_tables(size, rows):
    freq = np.arange(H)
    places = np.arange(size) - (size - 1) // 2
    right = np.zeros((N, N))
    right[:size] = np.concatenate(waves(freq[None, :], places[:, None]), 1)
    below = np.arange((size + 1) // 2)
    left = np.zeros((2, H, rows))
    left[:, :, : below.size] = waves(freq[:, None], below[None, :])
    left[:, :, 1:] *= 2.0
    return right, left[0], left[1]


def split(value):
    high = value.astype(jnp.bfloat16)
    low = (value - high.astype(jnp.float32)).astype(jnp.bfloat16)
    return high, low


def dot(left, right):
    return jnp.dot(left, right, preferred_element_type=jnp.float32)


def left(table, value):
    high, low = value
    return dot(table, jnp.concatenate([high, high, low], 0))


def right(value, table):
    high, low = value
    return dot(jnp.concatenate([high, high, low], 1), table)


def mix(f, p, q, rows):
    upper = slice(rows.start, rows.stop)
    lower = slice(H + rows.start, H + rows.stop)
    cc, cs, sc, ss = f[upper, :H], f[upper, H:], f[lower, :H], f[lower, H:]
    p, q = p[rows], q[rows]
    return p * cc + q * ss, p * cs - q * sc, p * sc - q * cs, p * ss + q * cc


def store_quarters(ref, rows, quarters):
    lower = slice(H + rows.start, H + rows.stop)
    places = ((rows, slice(0, H)), (rows, slice(H, N)), (lower, slice(0, H)), (lower, slice(H, N)))
    for (x, y), quarter in zip(places, quarters):
        ref[0, x, y], ref[1, x, y] = split(quarter)


CHUNKS = [slice(r, r + 16) for r in range(0, H, 16)]


def pipeline(count, *stages):
    for step in range(count + len(stages) - 1):
        for lag, stage in enumerate(reversed(stages)):
            item = step - (len(stages) - 1 - lag)
            if 0 <= item < count:
                stage(item)


def amplitudes(blocks, field, p_ref, q_ref, t, f_sc, g_sc, x_sc, a_sc, core):
    ey = split(right(split(field), t["fy"][...]))
    for b in range(blocks):
        rows = slice(b * H, b * H + N)
        f_sc[b] = left(t["fx"][...], (ey[0][rows], ey[1][rows]))

    def mixed(i):
        k, b = i // blocks, i % blocks
        for rows in CHUNKS:
            quarters = mix(f_sc.at[b], p_ref.at[k], q_ref.at[k], rows)
            store_quarters(g_sc.at[i], rows, quarters)

    def inverse_x(i):
        x = left(t["ix"][...], (g_sc[i, 0], g_sc[i, 1]))
        x_sc[0, i], x_sc[1, i] = split(x)

    def inverse_y(i):
        k, b = i // blocks, i % blocks
        a_sc[k, b * H : (b + 1) * H, :] = right((x_sc[0, i], x_sc[1, i]), t["iy_own"][core])

    pipeline(p_ref.shape[0] * blocks, mixed, inverse_x, inverse_y)


def slopes(blocks, count, a_sc, target, inside, w_sc):
    resists = []
    for c in range(0, blocks * H, R):
        rows = slice(c, c + R)
        amplitude = [a_sc[k, rows, :] for k in range(count)]
        total = amplitude[0] * amplitude[0]
        for k in range(1, count):
            total = total + amplitude[k] * amplitude[k]
        resist = 1.0 / (1.0 + jnp.exp(-STEEP * (total - THRESHOLD)))
        slope = 2.0 * (resist - target[rows]) * STEEP * resist * (1.0 - resist)
        slope = jnp.where(inside[rows], 2.0 * slope, 0.0)
        for k in range(count):
            cols = slice(k * H, (k + 1) * H)
            w_sc[0, rows, cols], w_sc[1, rows, cols] = split(amplitude[k] * slope)
        resists.append(resist)
    return resists


def gradients(blocks, count, p_ref, q_ref, t, w_sc, y_sc, u_sc, z_sc, core):
    def forward_x(b):
        rows = slice(b * H, b * H + N)
        y = left(t["fx"][...], (w_sc[0, rows, :], w_sc[1, rows, :]))
        y_sc[0, b], y_sc[1, b] = split(y)

    def forward_y(b):
        for k in range(count):
            cols = slice(k * H, (k + 1) * H)
            u_sc[b, k] = right((y_sc[0, b, :, cols], y_sc[1, b, :, cols]), t["fy_own"][core])

    def mixed(b):
        for rows in CHUNKS:
            terms = [mix(u_sc.at[b, k], p_ref.at[k], q_ref.at[k], rows) for k in range(count)]
            store_quarters(z_sc.at[b], rows, [sum(quarter) for quarter in zip(*terms)])

    def inverse_x(b):
        y_sc[0, b, :H, :N], y_sc[1, b, :H, :N] = split(left(t["ix"][...], (z_sc[b, 0], z_sc[b, 1])))

    out = []

    def inverse_y(b):
        out.append(right((y_sc[0, b, :H, :N], y_sc[1, b, :H, :N]), t["iy"][...]))

    pipeline(blocks, forward_x, forward_y, mixed, inverse_x, inverse_y)
    return out


def lane_mask(shape, core):
    lane = lax.broadcasted_iota(jnp.int32, shape, 1)
    return (lane >= core * R) & (lane < N - R + core * R)


def row_mask(shape, first, total):
    row = lax.broadcasted_iota(jnp.int32, shape, 0) + first
    return (row >= 0) & (row < total)


def spectrum_kernel(k_ref, right_ref, cos_ref, sin_ref, p_ref, q_ref):
    count = p_ref.shape[0]
    rows = k_ref.shape[0] // count
    section = right(split(k_ref[...]), right_ref[...])
    for k in range(count):
        high, low = split(section[k * rows : (k + 1) * rows])
        p_ref[k] = left(cos_ref[...], (high[:, :H], low[:, :H]))
        q_ref[k] = left(sin_ref[...], (high[:, H:], low[:, H:]))


TABLES = ("fx", "fy", "fy_own", "ix", "iy", "iy_own")


def first_kernel(tiles, near_ref, a1_ref, b1_ref, a2_ref, b2_ref, mate_ref, p_ref, q_ref, *refs):
    t = dict(zip(TABLES, refs))
    rest_ref, send_ref, target_ref, f_sc, g_sc, x_sc, a_sc, w_sc, y_sc, u_sc, z_sc = refs[len(TABLES) :]
    core, tile, total = lax.axis_index("gy"), lax.axis_index("gx"), tiles * H
    count = p_ref.shape[0]
    first = core == 0

    def ordered(*parts):
        pairs = zip(parts, parts[::-1])
        return jnp.concatenate([jnp.where(first, x, y) for x, y in pairs], 0)

    field = ordered(a2_ref[:H], a1_ref[:H], near_ref[:H], b1_ref[:H], b2_ref[:H])
    mate = [mate_ref[c * H : (c + 1) * H] for c in range(5)]
    mate = ordered(*mate[::-1])
    field = jnp.concatenate([jnp.where(first, field, mate), jnp.where(first, mate, field)], 1)
    inside = row_mask(field.shape, (tile - 2) * H, total) & lane_mask(field.shape, core)
    field = jnp.where(inside, field, 0.0)
    target = ordered(a2_ref[H:], a1_ref[H:], near_ref[H:], b1_ref[H:], b2_ref[H:])
    amplitudes(4, field, p_ref, q_ref, t, f_sc, g_sc, x_sc, a_sc, core)
    slopes(4, count, a_sc, target, row_mask((4 * H, H), (tile - 1) * H - R, total), w_sc)
    target_ref[...] = target[H : 3 * H]
    for b, part in enumerate(gradients(3, count, p_ref, q_ref, t, w_sc, y_sc, u_sc, z_sc, core)):
        rows = slice(b * H, (b + 1) * H)
        rest_ref[rows, :] = field[(b + 1) * H : (b + 2) * H] - STEP * part
        send_ref[rows, :] = pltpu.roll(part, N - R, 1)[:, :H]


def second_kernel(tiles, rest_ref, got_ref, target_ref, p_ref, q_ref, *refs):
    t = dict(zip(TABLES, refs))
    mask_ref, send_ref, resist_ref, f_sc, g_sc, x_sc, a_sc, w_sc, y_sc, u_sc, z_sc = refs[len(TABLES) :]
    core, tile, total = lax.axis_index("gy"), lax.axis_index("gx"), tiles * H
    count = p_ref.shape[0]
    got = jnp.concatenate([got_ref[...], jnp.zeros_like(got_ref)], 1)
    field = rest_ref[...] - STEP * pltpu.roll(got, R, 1)
    inside = row_mask(field.shape, (tile - 1) * H, total) & lane_mask(field.shape, core)
    field = jnp.where(inside, field, 0.0)
    amplitudes(2, field, p_ref, q_ref, t, f_sc, g_sc, x_sc, a_sc, core)
    inside = row_mask((2 * H, H), tile * H - R, total)
    resist = slopes(2, count, a_sc, target_ref[...], inside, w_sc)
    resist_ref[:R, :], resist_ref[R:, :] = resist[1], resist[2]
    (part,) = gradients(1, count, p_ref, q_ref, t, w_sc, y_sc, u_sc, z_sc, core)
    part = jnp.where(lane_mask(part.shape, core), STEP * part, 0.0)
    own = field[H : 2 * H] - part
    mask_ref[...] = jnp.where(core == 0, own[:, :H], own[:, H:])
    send_ref[...] = jnp.where(core == 0, part[:, H:], part[:, :H])


def shape(*dims, dtype=jnp.float32):
    return jax.ShapeDtypeStruct(dims, dtype)


def scratch(blocks, adjoint_blocks, count):
    items = count * blocks
    return [
        pltpu.VMEM((blocks, N, N), jnp.float32),
        pltpu.VMEM((items, 2, N, N), jnp.bfloat16),
        pltpu.VMEM((2, items, H, N), jnp.bfloat16),
        pltpu.VMEM((count, blocks * H, H), jnp.float32),
        pltpu.VMEM((2, blocks * H, count * H), jnp.bfloat16),
        pltpu.VMEM((2, adjoint_blocks, N, count * H), jnp.bfloat16),
        pltpu.VMEM((adjoint_blocks, count, N, N), jnp.float32),
        pltpu.VMEM((adjoint_blocks, 2, N, N), jnp.bfloat16),
    ]


def per_device(mask_init, target_map, kernels, tiles):
    count, size, _ = kernels.shape
    core = lax.axis_index("gy")
    tile = lax.axis_index("gx")
    swap = [(0, 1), (1, 0)]

    def ring(shift):
        pairs = []
        for x in range(tiles):
            for c, to in ((0, x + shift), (1, x - shift)):
                pairs.append((2 * x + c, 2 * to + c if 0 <= to < tiles else 2 * x + 1 - c))
        return pairs

    rows = 72
    half = jnp.pad(
        kernels[:, (size - 1) // 2 :, :],
        ((0, 0), (0, rows - (size + 1) // 2), (0, N - size)),
    ).reshape(count * rows, N)
    right_table, left_cos, left_sin = spectrum_tables(size, rows)
    spectral = [stack(right_table, 0), stack(left_cos, 1), stack(left_sin, 1)]
    spectral = [jnp.asarray(v) for v in spectral]
    p, q = pl.pallas_call(
        spectrum_kernel,
        out_shape=(shape(count, H, H), shape(count, H, H)),
        in_specs=[VMEM] * 4,
        out_specs=(VMEM, VMEM),
        cost_estimate=pl.CostEstimate(
            flops=6 * count * rows * N * N * 4, bytes_accessed=4 * count * N * N, transcendentals=0
        ),
        compiler_params=pltpu.CompilerParams(vmem_limit_bytes=12 << 20),
        name="spectra",
    )(half, *spectral)

    forward, inverse = wave_tables()
    halves = [slice(c, c + H) for c in (0, H)]
    tables = [
        stack(forward, 1),
        stack(forward.T, 0),
        np.stack([stack(forward.T[c], 0) for c in halves]),
        stack(inverse[R : R + H], 1),
        stack(inverse.T, 0),
        np.stack([stack(inverse.T[:, c], 0) for c in halves]),
    ]
    tables = [jnp.asarray(v) for v in tables]

    near = jnp.concatenate([mask_init, target_map.astype(jnp.float32)], 0)
    first, second = near[H : H + R], near[H + R :]
    up = jnp.concatenate([near[:H], jnp.where(core == 0, second, first)], 0)
    down = jnp.concatenate([near[:H], jnp.where(core == 0, first, second)], 0)
    both = ("gx", "gy")
    around = [
        lax.ppermute(near, both, ring(1)),
        lax.ppermute(near, both, ring(-1)),
        lax.ppermute(up, both, ring(2)),
        lax.ppermute(down, both, ring(-2)),
    ]
    *around, p, q = lax.optimization_barrier((*around, p, q))
    a1, b1, a2, b2 = around
    mate = lax.ppermute(
        jnp.concatenate([a2[:H], a1[:H], near[:H], b1[:H], b2[:H]], 0), "gy", swap
    )

    params = pltpu.CompilerParams(vmem_limit_bytes=40 << 20)
    rest, send, target = pl.pallas_call(
        functools.partial(first_kernel, tiles),
        out_shape=(shape(3 * H, N), shape(3 * H, H), shape(2 * H, H)),
        in_specs=[VMEM] * (8 + len(tables)),
        out_specs=(VMEM,) * 3,
        scratch_shapes=scratch(4, 3, count),
        compiler_params=params,
        name="first_step",
    )(near, a1, b1, a2, b2, mate, p, q, *tables)
    got = lax.ppermute(send, "gy", swap)
    mask, send, resist = pl.pallas_call(
        functools.partial(second_kernel, tiles),
        out_shape=(shape(H, H), shape(H, H), shape(H, H)),
        in_specs=[VMEM] * (5 + len(tables)),
        out_specs=(VMEM,) * 3,
        scratch_shapes=scratch(2, 1, count),
        compiler_params=params,
        name="second_step",
    )(rest, got, target, p, q, *tables)
    return mask - lax.ppermute(send, "gy", swap), resist


def solution(mesh):
    spec = P(("win", "gx"), "gy")
    return jax.shard_map(
        functools.partial(per_device, tiles=mesh.shape["gx"]),
        mesh=mesh,
        in_specs=(spec, spec, P()),
        out_specs=(spec, spec),
        check_vma=False,
    )
```

```python
import functools

import jax
import jax.numpy as jnp
import ml_dtypes
import numpy as np
from jax import lax
from jax.experimental import pallas as pl
from jax.experimental.pallas import tpu as pltpu
from jax.sharding import PartitionSpec as P

STEP = 0.1
STEEP = 4.0
THRESHOLD = 1.5
N = 256
H = 128
R = 64
VMEM = pl.BlockSpec(memory_space=pltpu.VMEM)


def stack(table, axis):
    high = table.astype(ml_dtypes.bfloat16)
    low = (table - high.astype(np.float64)).astype(ml_dtypes.bfloat16)
    return np.concatenate([high, low, high], axis)


def waves(freqs, places):
    angle = np.pi / N * ((2 * freqs + 1) * places % (2 * N))
    return np.cos(angle), np.sin(angle)


def wave_tables():
    forward = np.concatenate(waves(np.arange(H)[:, None], np.arange(N)[None, :]), 0)
    return forward, forward.T * (2.0 / N)


def spectrum_tables(size, rows):
    freq = np.arange(H)
    places = np.arange(size) - (size - 1) // 2
    right = np.zeros((N, N))
    right[:size] = np.concatenate(waves(freq[None, :], places[:, None]), 1)
    below = np.arange((size + 1) // 2)
    left = np.zeros((2, H, rows))
    left[:, :, : below.size] = waves(freq[:, None], below[None, :])
    left[:, :, 1:] *= 2.0
    return right, left[0], left[1]


def split(value):
    high = value.astype(jnp.bfloat16)
    low = (value - high.astype(jnp.float32)).astype(jnp.bfloat16)
    return high, low


def dot(left, right):
    return jnp.dot(left, right, preferred_element_type=jnp.float32)


def left(table, value):
    high, low = value
    return dot(table, jnp.concatenate([high, high, low], 0))


def right(value, table):
    high, low = value
    return dot(jnp.concatenate([high, high, low], 1), table)


def mix(f, p, q, rows):
    upper = slice(rows.start, rows.stop)
    lower = slice(H + rows.start, H + rows.stop)
    cc, cs, sc, ss = f[upper, :H], f[upper, H:], f[lower, :H], f[lower, H:]
    p, q = p[rows], q[rows]
    return p * cc + q * ss, p * cs - q * sc, p * sc - q * cs, p * ss + q * cc


def store_quarters(ref, rows, quarters):
    lower = slice(H + rows.start, H + rows.stop)
    places = ((rows, slice(0, H)), (rows, slice(H, N)), (lower, slice(0, H)), (lower, slice(H, N)))
    for (x, y), quarter in zip(places, quarters):
        ref[0, x, y], ref[1, x, y] = split(quarter)


CHUNKS = [slice(r, r + 16) for r in range(0, H, 16)]


def pipeline(count, *stages):
    for step in range(count + 2 * (len(stages) - 1)):
        for place, stage in enumerate(stages):
            item = step - 2 * place
            if 0 <= item < count:
                stage(item)


def amplitudes(blocks, count, field, p_ref, q_ref, t, f_sc, g_sc, x_sc, a_sc, core, ready):
    ey = split(right(split(field), t["fy"][...]))
    for b in range(blocks):
        rows = slice(b * H, b * H + N)
        f_sc[b] = left(t["fx"][...], (ey[0][rows], ey[1][rows]))

    def mixed(i):
        b, k = i // count, i % count
        for rows in CHUNKS:
            quarters = mix(f_sc.at[b], p_ref.at[k], q_ref.at[k], rows)
            store_quarters(g_sc.at[i], rows, quarters)

    def inverse_x(i):
        x = left(t["ix"][...], (g_sc[i, 0], g_sc[i, 1]))
        x_sc[0, i], x_sc[1, i] = split(x)

    def inverse_y(i):
        b, k = i // count, i % count
        a_sc[k, b * H : (b + 1) * H, :] = right((x_sc[0, i], x_sc[1, i]), t["iy_own"][core])
        if k == count - 1:
            ready(b)

    pipeline(count * blocks, mixed, inverse_x, inverse_y)


def slopes(b, count, a_sc, target, inside, w_sc):
    resists = []
    for c in range(b * H, (b + 1) * H, R):
        rows = slice(c, c + R)
        amplitude = [a_sc[k, rows, :] for k in range(count)]
        total = amplitude[0] * amplitude[0]
        for k in range(1, count):
            total = total + amplitude[k] * amplitude[k]
        resist = 1.0 / (1.0 + jnp.exp(-STEEP * (total - THRESHOLD)))
        slope = 2.0 * (resist - target[rows]) * STEEP * resist * (1.0 - resist)
        slope = jnp.where(inside[rows], 2.0 * slope, 0.0)
        for k in range(count):
            cols = slice(k * H, (k + 1) * H)
            w_sc[0, rows, cols], w_sc[1, rows, cols] = split(amplitude[k] * slope)
        resists.append(resist)
    return resists


def gradients(blocks, count, p_ref, q_ref, t, w_sc, y_sc, u_sc, z_sc, core):
    def forward_x(b):
        rows = slice(b * H, b * H + N)
        y = left(t["fx"][...], (w_sc[0, rows, :], w_sc[1, rows, :]))
        y_sc[0, b], y_sc[1, b] = split(y)

    def forward_y(b):
        for k in range(count):
            cols = slice(k * H, (k + 1) * H)
            u_sc[b, k] = right((y_sc[0, b, :, cols], y_sc[1, b, :, cols]), t["fy_own"][core])

    def mixed(b):
        for rows in CHUNKS:
            terms = [mix(u_sc.at[b, k], p_ref.at[k], q_ref.at[k], rows) for k in range(count)]
            store_quarters(z_sc.at[b], rows, [sum(quarter) for quarter in zip(*terms)])

    def inverse_x(b):
        y_sc[0, b, :H, :N], y_sc[1, b, :H, :N] = split(left(t["ix"][...], (z_sc[b, 0], z_sc[b, 1])))

    out = []

    def inverse_y(b):
        out.append(right((y_sc[0, b, :H, :N], y_sc[1, b, :H, :N]), t["iy"][...]))

    pipeline(blocks, forward_x, forward_y, mixed, inverse_x, inverse_y)
    return out


def lane_mask(shape, core):
    lane = lax.broadcasted_iota(jnp.int32, shape, 1)
    return (lane >= core * R) & (lane < N - R + core * R)


def row_mask(shape, first, total):
    row = lax.broadcasted_iota(jnp.int32, shape, 0) + first
    return (row >= 0) & (row < total)


def spectrum_kernel(k_ref, right_ref, cos_ref, sin_ref, p_ref, q_ref):
    count = p_ref.shape[0]
    rows = k_ref.shape[0] // count
    section = right(split(k_ref[...]), right_ref[...])
    for k in range(count):
        high, low = split(section[k * rows : (k + 1) * rows])
        p_ref[k] = left(cos_ref[...], (high[:, :H], low[:, :H]))
        q_ref[k] = left(sin_ref[...], (high[:, H:], low[:, H:]))


TABLES = ("fx", "fy", "fy_own", "ix", "iy", "iy_own")


def first_kernel(tiles, near_ref, a1_ref, b1_ref, a2_ref, b2_ref, mate_ref, p_ref, q_ref, *refs):
    t = dict(zip(TABLES, refs))
    rest_ref, send_ref, target_ref, f_sc, g_sc, x_sc, a_sc, w_sc, y_sc, u_sc, z_sc = refs[len(TABLES) :]
    core, tile, total = lax.axis_index("gy"), lax.axis_index("gx"), tiles * H
    count = p_ref.shape[0]
    first = core == 0

    def ordered(*parts):
        pairs = zip(parts, parts[::-1])
        return jnp.concatenate([jnp.where(first, x, y) for x, y in pairs], 0)

    field = ordered(a2_ref[:H], a1_ref[:H], near_ref[:H], b1_ref[:H], b2_ref[:H])
    mate = [mate_ref[c * H : (c + 1) * H] for c in range(5)]
    mate = ordered(*mate[::-1])
    field = jnp.concatenate([jnp.where(first, field, mate), jnp.where(first, mate, field)], 1)
    inside = row_mask(field.shape, (tile - 2) * H, total) & lane_mask(field.shape, core)
    field = jnp.where(inside, field, 0.0)
    target = ordered(a2_ref[H:], a1_ref[H:], near_ref[H:], b1_ref[H:], b2_ref[H:])
    inside = row_mask((4 * H, H), (tile - 1) * H - R, total)

    def ready(b):
        slopes(b, count, a_sc, target, inside, w_sc)

    amplitudes(4, count, field, p_ref, q_ref, t, f_sc, g_sc, x_sc, a_sc, core, ready)
    target_ref[...] = target[H : 3 * H]
    for b, part in enumerate(gradients(3, count, p_ref, q_ref, t, w_sc, y_sc, u_sc, z_sc, core)):
        rows = slice(b * H, (b + 1) * H)
        rest_ref[rows, :] = field[(b + 1) * H : (b + 2) * H] - STEP * part
        send_ref[rows, :] = pltpu.roll(part, N - R, 1)[:, :H]


def second_kernel(tiles, rest_ref, got_ref, target_ref, p_ref, q_ref, *refs):
    t = dict(zip(TABLES, refs))
    mask_ref, send_ref, resist_ref, f_sc, g_sc, x_sc, a_sc, w_sc, y_sc, u_sc, z_sc = refs[len(TABLES) :]
    core, tile, total = lax.axis_index("gy"), lax.axis_index("gx"), tiles * H
    count = p_ref.shape[0]
    got = jnp.concatenate([got_ref[...], jnp.zeros_like(got_ref)], 1)
    field = rest_ref[...] - STEP * pltpu.roll(got, R, 1)
    inside = row_mask(field.shape, (tile - 1) * H, total) & lane_mask(field.shape, core)
    field = jnp.where(inside, field, 0.0)
    inside = row_mask((2 * H, H), tile * H - R, total)
    target = target_ref[...]

    def ready(b):
        resist = slopes(b, count, a_sc, target, inside, w_sc)
        resist_ref[b * R : (b + 1) * R, :] = resist[1 - b]

    amplitudes(2, count, field, p_ref, q_ref, t, f_sc, g_sc, x_sc, a_sc, core, ready)
    (part,) = gradients(1, count, p_ref, q_ref, t, w_sc, y_sc, u_sc, z_sc, core)
    part = jnp.where(lane_mask(part.shape, core), STEP * part, 0.0)
    own = field[H : 2 * H] - part
    mask_ref[...] = jnp.where(core == 0, own[:, :H], own[:, H:])
    send_ref[...] = jnp.where(core == 0, part[:, H:], part[:, :H])


def shape(*dims, dtype=jnp.float32):
    return jax.ShapeDtypeStruct(dims, dtype)


def scratch(blocks, adjoint_blocks, count):
    items = count * blocks
    return [
        pltpu.VMEM((blocks, N, N), jnp.float32),
        pltpu.VMEM((items, 2, N, N), jnp.bfloat16),
        pltpu.VMEM((2, items, H, N), jnp.bfloat16),
        pltpu.VMEM((count, blocks * H, H), jnp.float32),
        pltpu.VMEM((2, blocks * H, count * H), jnp.bfloat16),
        pltpu.VMEM((2, adjoint_blocks, N, count * H), jnp.bfloat16),
        pltpu.VMEM((adjoint_blocks, count, N, N), jnp.float32),
        pltpu.VMEM((adjoint_blocks, 2, N, N), jnp.bfloat16),
    ]


def per_device(mask_init, target_map, kernels, tiles):
    count, size, _ = kernels.shape
    core = lax.axis_index("gy")
    tile = lax.axis_index("gx")
    swap = [(0, 1), (1, 0)]

    def ring(shift):
        pairs = []
        for x in range(tiles):
            for c, to in ((0, x + shift), (1, x - shift)):
                pairs.append((2 * x + c, 2 * to + c if 0 <= to < tiles else 2 * x + 1 - c))
        return pairs

    rows = 72
    half = jnp.pad(
        kernels[:, (size - 1) // 2 :, :],
        ((0, 0), (0, rows - (size + 1) // 2), (0, N - size)),
    ).reshape(count * rows, N)
    right_table, left_cos, left_sin = spectrum_tables(size, rows)
    spectral = [stack(right_table, 0), stack(left_cos, 1), stack(left_sin, 1)]
    spectral = [jnp.asarray(v) for v in spectral]
    p, q = pl.pallas_call(
        spectrum_kernel,
        out_shape=(shape(count, H, H), shape(count, H, H)),
        in_specs=[VMEM] * 4,
        out_specs=(VMEM, VMEM),
        cost_estimate=pl.CostEstimate(
            flops=6 * count * rows * N * N * 4, bytes_accessed=4 * count * N * N, transcendentals=0
        ),
        compiler_params=pltpu.CompilerParams(vmem_limit_bytes=12 << 20),
        name="spectra",
    )(half, *spectral)

    forward, inverse = wave_tables()
    halves = [slice(c, c + H) for c in (0, H)]
    tables = [
        stack(forward, 1),
        stack(forward.T, 0),
        np.stack([stack(forward.T[c], 0) for c in halves]),
        stack(inverse[R : R + H], 1),
        stack(inverse.T, 0),
        np.stack([stack(inverse.T[:, c], 0) for c in halves]),
    ]
    tables = [jnp.asarray(v) for v in tables]

    near = jnp.concatenate([mask_init, target_map.astype(jnp.float32)], 0)
    first, second = near[H : H + R], near[H + R :]
    up = jnp.concatenate([near[:H], jnp.where(core == 0, second, first)], 0)
    down = jnp.concatenate([near[:H], jnp.where(core == 0, first, second)], 0)
    both = ("gx", "gy")
    around = [
        lax.ppermute(near, both, ring(1)),
        lax.ppermute(near, both, ring(-1)),
        lax.ppermute(up, both, ring(2)),
        lax.ppermute(down, both, ring(-2)),
    ]
    *around, p, q = lax.optimization_barrier((*around, p, q))
    a1, b1, a2, b2 = around
    mate = lax.ppermute(
        jnp.concatenate([a2[:H], a1[:H], near[:H], b1[:H], b2[:H]], 0), "gy", swap
    )

    params = pltpu.CompilerParams(vmem_limit_bytes=40 << 20)
    rest, send, target = pl.pallas_call(
        functools.partial(first_kernel, tiles),
        out_shape=(shape(3 * H, N), shape(3 * H, H), shape(2 * H, H)),
        in_specs=[VMEM] * (8 + len(tables)),
        out_specs=(VMEM,) * 3,
        scratch_shapes=scratch(4, 3, count),
        compiler_params=params,
        name="first_step",
    )(near, a1, b1, a2, b2, mate, p, q, *tables)
    got = lax.ppermute(send, "gy", swap)
    mask, send, resist = pl.pallas_call(
        functools.partial(second_kernel, tiles),
        out_shape=(shape(H, H), shape(H, H), shape(H, H)),
        in_specs=[VMEM] * (5 + len(tables)),
        out_specs=(VMEM,) * 3,
        scratch_shapes=scratch(2, 1, count),
        compiler_params=params,
        name="second_step",
    )(rest, got, target, p, q, *tables)
    return mask - lax.ppermute(send, "gy", swap), resist


def solution(mesh):
    spec = P(("win", "gx"), "gy")
    return jax.shard_map(
        functools.partial(per_device, tiles=mesh.shape["gx"]),
        mesh=mesh,
        in_specs=(spec, spec, P()),
        out_specs=(spec, spec),
        check_vma=False,
    )
```

```python
import functools

import jax
import jax.numpy as jnp
import ml_dtypes
import numpy as np
from jax import lax
from jax.experimental import pallas as pl
from jax.experimental.pallas import tpu as pltpu
from jax.sharding import PartitionSpec as P

STEP = 0.1
STEEP = 4.0
THRESHOLD = 1.5
N = 256
H = 128
R = 64
VMEM = pl.BlockSpec(memory_space=pltpu.VMEM)


def stack(table, axis):
    high = table.astype(ml_dtypes.bfloat16)
    low = (table - high.astype(np.float64)).astype(ml_dtypes.bfloat16)
    return np.concatenate([high, low, high], axis)


def waves(freqs, places):
    angle = np.pi / N * ((2 * freqs + 1) * places % (2 * N))
    return np.cos(angle), np.sin(angle)


def wave_tables():
    forward = np.concatenate(waves(np.arange(H)[:, None], np.arange(N)[None, :]), 0)
    return forward, forward.T * (2.0 / N)


def spectrum_tables(size, rows):
    freq = np.arange(H)
    places = np.arange(size) - (size - 1) // 2
    right = np.zeros((N, N))
    right[:size] = np.concatenate(waves(freq[None, :], places[:, None]), 1)
    below = np.arange((size + 1) // 2)
    left = np.zeros((2, H, rows))
    left[:, :, : below.size] = waves(freq[:, None], below[None, :])
    left[:, :, 1:] *= 2.0
    return right, left[0], left[1]


def split(value):
    high = value.astype(jnp.bfloat16)
    low = (value - high.astype(jnp.float32)).astype(jnp.bfloat16)
    return high, low


def dot(left, right):
    return jnp.dot(left, right, preferred_element_type=jnp.float32)


def left(table, value):
    high, low = value
    return dot(table, jnp.concatenate([high, high, low], 0))


def right(value, table):
    high, low = value
    return dot(jnp.concatenate([high, high, low], 1), table)


def mix(f, p, q, rows):
    upper = slice(rows.start, rows.stop)
    lower = slice(H + rows.start, H + rows.stop)
    cc, cs, sc, ss = f[upper, :H], f[upper, H:], f[lower, :H], f[lower, H:]
    p, q = p[rows], q[rows]
    return p * cc + q * ss, p * cs - q * sc, p * sc - q * cs, p * ss + q * cc


def store_quarters(ref, rows, quarters):
    lower = slice(H + rows.start, H + rows.stop)
    places = ((rows, slice(0, H)), (rows, slice(H, N)), (lower, slice(0, H)), (lower, slice(H, N)))
    for (x, y), quarter in zip(places, quarters):
        ref[0, x, y], ref[1, x, y] = split(quarter)


CHUNKS = [slice(r, r + 16) for r in range(0, H, 16)]


def pipeline(count, *stages):
    lag = 1 if count <= 12 else 2
    for step in range(count + lag * (len(stages) - 1)):
        for place, stage in enumerate(stages):
            item = step - lag * place
            if 0 <= item < count:
                stage(item)


def amplitudes(blocks, count, field, p_ref, q_ref, t, f_sc, g_sc, x_sc, a_sc, core, ready):
    ey = split(right(split(field), t["fy"][...]))
    for b in range(blocks):
        rows = slice(b * H, b * H + N)
        f_sc[b] = left(t["fx"][...], (ey[0][rows], ey[1][rows]))

    def mixed(i):
        b, k = i // count, i % count
        for rows in CHUNKS:
            quarters = mix(f_sc.at[b], p_ref.at[k], q_ref.at[k], rows)
            store_quarters(g_sc.at[i], rows, quarters)

    def inverse_x(i):
        x = left(t["ix"][...], (g_sc[i, 0], g_sc[i, 1]))
        x_sc[0, i], x_sc[1, i] = split(x)

    def inverse_y(i):
        b, k = i // count, i % count
        a_sc[k, b * H : (b + 1) * H, :] = right((x_sc[0, i], x_sc[1, i]), t["iy_own"][core])
        if k == count - 1:
            ready(b)

    pipeline(count * blocks, mixed, inverse_x, inverse_y)


def slopes(b, count, a_sc, target, inside, w_sc):
    resists = []
    for c in range(b * H, (b + 1) * H, R):
        rows = slice(c, c + R)
        amplitude = [a_sc[k, rows, :] for k in range(count)]
        total = amplitude[0] * amplitude[0]
        for k in range(1, count):
            total = total + amplitude[k] * amplitude[k]
        resist = 1.0 / (1.0 + jnp.exp(-STEEP * (total - THRESHOLD)))
        slope = 2.0 * (resist - target[rows]) * STEEP * resist * (1.0 - resist)
        slope = jnp.where(inside[rows], 2.0 * slope, 0.0)
        for k in range(count):
            cols = slice(k * H, (k + 1) * H)
            w_sc[0, rows, cols], w_sc[1, rows, cols] = split(amplitude[k] * slope)
        resists.append(resist)
    return resists


def gradients(blocks, count, p_ref, q_ref, t, w_sc, y_sc, u_sc, z_sc, core):
    def forward_x(b):
        rows = slice(b * H, b * H + N)
        y = left(t["fx"][...], (w_sc[0, rows, :], w_sc[1, rows, :]))
        y_sc[0, b], y_sc[1, b] = split(y)

    def forward_y(b):
        for k in range(count):
            cols = slice(k * H, (k + 1) * H)
            u_sc[b, k] = right((y_sc[0, b, :, cols], y_sc[1, b, :, cols]), t["fy_own"][core])

    def mixed(b):
        for rows in CHUNKS:
            terms = [mix(u_sc.at[b, k], p_ref.at[k], q_ref.at[k], rows) for k in range(count)]
            store_quarters(z_sc.at[b], rows, [sum(quarter) for quarter in zip(*terms)])

    def inverse_x(b):
        y_sc[0, b, :H, :N], y_sc[1, b, :H, :N] = split(left(t["ix"][...], (z_sc[b, 0], z_sc[b, 1])))

    out = []

    def inverse_y(b):
        out.append(right((y_sc[0, b, :H, :N], y_sc[1, b, :H, :N]), t["iy"][...]))

    pipeline(blocks, forward_x, forward_y, mixed, inverse_x, inverse_y)
    return out


def lane_mask(shape, core):
    lane = lax.broadcasted_iota(jnp.int32, shape, 1)
    return (lane >= core * R) & (lane < N - R + core * R)


def row_mask(shape, first, total):
    row = lax.broadcasted_iota(jnp.int32, shape, 0) + first
    return (row >= 0) & (row < total)


def spectrum_kernel(k_ref, right_ref, cos_ref, sin_ref, p_ref, q_ref):
    count = p_ref.shape[0]
    rows = k_ref.shape[0] // count
    section = right(split(k_ref[...]), right_ref[...])
    for k in range(count):
        high, low = split(section[k * rows : (k + 1) * rows])
        p_ref[k] = left(cos_ref[...], (high[:, :H], low[:, :H]))
        q_ref[k] = left(sin_ref[...], (high[:, H:], low[:, H:]))


TABLES = ("fx", "fy", "fy_own", "ix", "iy", "iy_own")


def first_kernel(tiles, near_ref, a1_ref, b1_ref, a2_ref, b2_ref, mate_ref, p_ref, q_ref, *refs):
    t = dict(zip(TABLES, refs))
    rest_ref, send_ref, target_ref, f_sc, g_sc, x_sc, a_sc, w_sc, y_sc, u_sc, z_sc = refs[len(TABLES) :]
    core, tile, total = lax.axis_index("gy"), lax.axis_index("gx"), tiles * H
    count = p_ref.shape[0]
    first = core == 0

    def ordered(*parts):
        pairs = zip(parts, parts[::-1])
        return jnp.concatenate([jnp.where(first, x, y) for x, y in pairs], 0)

    field = ordered(a2_ref[:H], a1_ref[:H], near_ref[:H], b1_ref[:H], b2_ref[:H])
    mate = [mate_ref[c * H : (c + 1) * H] for c in range(5)]
    mate = ordered(*mate[::-1])
    field = jnp.concatenate([jnp.where(first, field, mate), jnp.where(first, mate, field)], 1)
    inside = row_mask(field.shape, (tile - 2) * H, total) & lane_mask(field.shape, core)
    field = jnp.where(inside, field, 0.0)
    target = ordered(a2_ref[H:], a1_ref[H:], near_ref[H:], b1_ref[H:], b2_ref[H:])
    inside = row_mask((4 * H, H), (tile - 1) * H - R, total)

    def ready(b):
        slopes(b, count, a_sc, target, inside, w_sc)

    amplitudes(4, count, field, p_ref, q_ref, t, f_sc, g_sc, x_sc, a_sc, core, ready)
    target_ref[...] = target[H : 3 * H]
    for b, part in enumerate(gradients(3, count, p_ref, q_ref, t, w_sc, y_sc, u_sc, z_sc, core)):
        rows = slice(b * H, (b + 1) * H)
        rest_ref[rows, :] = field[(b + 1) * H : (b + 2) * H] - STEP * part
        send_ref[rows, :] = pltpu.roll(part, N - R, 1)[:, :H]


def second_kernel(tiles, rest_ref, got_ref, target_ref, p_ref, q_ref, *refs):
    t = dict(zip(TABLES, refs))
    mask_ref, send_ref, resist_ref, f_sc, g_sc, x_sc, a_sc, w_sc, y_sc, u_sc, z_sc = refs[len(TABLES) :]
    core, tile, total = lax.axis_index("gy"), lax.axis_index("gx"), tiles * H
    count = p_ref.shape[0]
    got = jnp.concatenate([got_ref[...], jnp.zeros_like(got_ref)], 1)
    field = rest_ref[...] - STEP * pltpu.roll(got, R, 1)
    inside = row_mask(field.shape, (tile - 1) * H, total) & lane_mask(field.shape, core)
    field = jnp.where(inside, field, 0.0)
    inside = row_mask((2 * H, H), tile * H - R, total)
    target = target_ref[...]

    def ready(b):
        resist = slopes(b, count, a_sc, target, inside, w_sc)
        resist_ref[b * R : (b + 1) * R, :] = resist[1 - b]

    amplitudes(2, count, field, p_ref, q_ref, t, f_sc, g_sc, x_sc, a_sc, core, ready)
    (part,) = gradients(1, count, p_ref, q_ref, t, w_sc, y_sc, u_sc, z_sc, core)
    part = jnp.where(lane_mask(part.shape, core), STEP * part, 0.0)
    own = field[H : 2 * H] - part
    mask_ref[...] = jnp.where(core == 0, own[:, :H], own[:, H:])
    send_ref[...] = jnp.where(core == 0, part[:, H:], part[:, :H])


def shape(*dims, dtype=jnp.float32):
    return jax.ShapeDtypeStruct(dims, dtype)


def scratch(blocks, adjoint_blocks, count):
    items = count * blocks
    return [
        pltpu.VMEM((blocks, N, N), jnp.float32),
        pltpu.VMEM((items, 2, N, N), jnp.bfloat16),
        pltpu.VMEM((2, items, H, N), jnp.bfloat16),
        pltpu.VMEM((count, blocks * H, H), jnp.float32),
        pltpu.VMEM((2, blocks * H, count * H), jnp.bfloat16),
        pltpu.VMEM((2, adjoint_blocks, N, count * H), jnp.bfloat16),
        pltpu.VMEM((adjoint_blocks, count, N, N), jnp.float32),
        pltpu.VMEM((adjoint_blocks, 2, N, N), jnp.bfloat16),
    ]


def per_device(mask_init, target_map, kernels, tiles):
    count, size, _ = kernels.shape
    core = lax.axis_index("gy")
    tile = lax.axis_index("gx")
    swap = [(0, 1), (1, 0)]

    def ring(shift):
        pairs = []
        for x in range(tiles):
            for c, to in ((0, x + shift), (1, x - shift)):
                pairs.append((2 * x + c, 2 * to + c if 0 <= to < tiles else 2 * x + 1 - c))
        return pairs

    rows = 72
    half = jnp.pad(
        kernels[:, (size - 1) // 2 :, :],
        ((0, 0), (0, rows - (size + 1) // 2), (0, N - size)),
    ).reshape(count * rows, N)
    right_table, left_cos, left_sin = spectrum_tables(size, rows)
    spectral = [stack(right_table, 0), stack(left_cos, 1), stack(left_sin, 1)]
    spectral = [jnp.asarray(v) for v in spectral]
    p, q = pl.pallas_call(
        spectrum_kernel,
        out_shape=(shape(count, H, H), shape(count, H, H)),
        in_specs=[VMEM] * 4,
        out_specs=(VMEM, VMEM),
        cost_estimate=pl.CostEstimate(
            flops=6 * count * rows * N * N * 4, bytes_accessed=4 * count * N * N, transcendentals=0
        ),
        compiler_params=pltpu.CompilerParams(vmem_limit_bytes=12 << 20),
        name="spectra",
    )(half, *spectral)

    forward, inverse = wave_tables()
    halves = [slice(c, c + H) for c in (0, H)]
    tables = [
        stack(forward, 1),
        stack(forward.T, 0),
        np.stack([stack(forward.T[c], 0) for c in halves]),
        stack(inverse[R : R + H], 1),
        stack(inverse.T, 0),
        np.stack([stack(inverse.T[:, c], 0) for c in halves]),
    ]
    tables = [jnp.asarray(v) for v in tables]

    near = jnp.concatenate([mask_init, target_map.astype(jnp.float32)], 0)
    first, second = near[H : H + R], near[H + R :]
    up = jnp.concatenate([near[:H], jnp.where(core == 0, second, first)], 0)
    down = jnp.concatenate([near[:H], jnp.where(core == 0, first, second)], 0)
    both = ("gx", "gy")
    around = [
        lax.ppermute(near, both, ring(1)),
        lax.ppermute(near, both, ring(-1)),
        lax.ppermute(up, both, ring(2)),
        lax.ppermute(down, both, ring(-2)),
    ]
    *around, p, q = lax.optimization_barrier((*around, p, q))
    a1, b1, a2, b2 = around
    mate = lax.ppermute(
        jnp.concatenate([a2[:H], a1[:H], near[:H], b1[:H], b2[:H]], 0), "gy", swap
    )

    params = pltpu.CompilerParams(vmem_limit_bytes=40 << 20)
    rest, send, target = pl.pallas_call(
        functools.partial(first_kernel, tiles),
        out_shape=(shape(3 * H, N), shape(3 * H, H), shape(2 * H, H)),
        in_specs=[VMEM] * (8 + len(tables)),
        out_specs=(VMEM,) * 3,
        scratch_shapes=scratch(4, 3, count),
        compiler_params=params,
        name="first_step",
    )(near, a1, b1, a2, b2, mate, p, q, *tables)
    got = lax.ppermute(send, "gy", swap)
    mask, send, resist = pl.pallas_call(
        functools.partial(second_kernel, tiles),
        out_shape=(shape(H, H), shape(H, H), shape(H, H)),
        in_specs=[VMEM] * (5 + len(tables)),
        out_specs=(VMEM,) * 3,
        scratch_shapes=scratch(2, 1, count),
        compiler_params=params,
        name="second_step",
    )(rest, got, target, p, q, *tables)
    return mask - lax.ppermute(send, "gy", swap), resist


def solution(mesh):
    spec = P(("win", "gx"), "gy")
    return jax.shard_map(
        functools.partial(per_device, tiles=mesh.shape["gx"]),
        mesh=mesh,
        in_specs=(spec, spec, P()),
        out_specs=(spec, spec),
        check_vma=False,
    )
```
